32 devices in a mesh: rows: 32 (over z, y, x, core).
Axes of the slice: x: 2, y: 2, z: 4, core: 2. Of those that a mesh axis runs over, the one named last changes fastest.
Arguments:
- snapshots: float32 [262144, 128], P('rows')
- send_list: int32 [1024, 64], P('rows'), may hold values from 0 to 8191
- stencil: int32 [524288, 8], P('rows'), may hold values from 0 to 2047, as said below
- weights: float32 [524288, 8], P('rows'), may hold values from 0.2 to 1
Outputs:
- basis: float32 [524288, 128], P('rows')
- r_factor: float32 [128, 128], replicated
The draws below stay inside these ranges and needn't reach their ends.
Inputs may be any that keep to these rules, and one draw needn't show every extreme that they name: `send_list`: every slot carries a node; a node may fill several slots. `stencil`: all 8 donors of a row lie on one peer: local row k of device d takes them from peer (d + k // 512) mod 32. Every slot that a device receives is read by some of its rows.
All inputs are finite; a program needn't handle non-finite values.
Results may differ from the reference program's by a relative error of at most 0.0003.
Values sent between devices are 32-bit elements; how exact they have to be, the bound alone decides.
No kernel may reach another device: no remote copies, remote signals or barrier semaphores. Data moves between devices by JAX's collectives and lax.ppermute only.
A program may use at most 192 MiB of HBM per device.

```python
import math
import jax
import jax.numpy as jnp
from jax import lax

SNAPS = 128
STENCIL = 8
NODE_DEV = 8192
ROW_DEV = 16384
CAP = 64
NODES = 262144
ROWS = 524288
N_ROWS = 32


def mode_table(count):
    mode = jnp.arange(count, dtype=jnp.int32)[:, None]
    instant = jnp.arange(count, dtype=jnp.int32)[None, :]
    freq = (mode + 1) // 2
    phase = freq * instant % count
    angle = phase.astype(jnp.float32) * (2.0 * math.pi / count)
    middle = jnp.where(mode % 2 == 1, jnp.cos(angle), jnp.sin(angle)) * math.sqrt(2.0 / count)
    first = jnp.full((1, count), 1.0 / math.sqrt(count), jnp.float32)
    last = jnp.where(instant % 2 == 0, 1.0, -1.0).astype(jnp.float32) / math.sqrt(count)
    return jnp.concatenate([first, middle[1:count - 1], last], axis=0).astype(jnp.float32)


def draw_snapshots(key, part):
    k1, k2 = jax.random.split(key, 2)
    order = jax.random.permutation(k1, SNAPS).astype(jnp.float32)
    gains = 3.0 * jnp.exp(-math.log(300.0) * order / (SNAPS - 1))
    noise = jax.random.normal(k2, (NODES, SNAPS), jnp.float32)
    values = jnp.dot(noise * gains[None, :], mode_table(SNAPS), precision=lax.Precision.HIGHEST, preferred_element_type=jnp.float32)
    return values.astype(jnp.float32)


def draw_stencil(key, part):
    k1, k2 = jax.random.split(key)
    run_rows = ROW_DEV // N_ROWS
    rowid = jnp.arange(ROWS, dtype=jnp.int32)
    owner = rowid // ROW_DEV
    local = rowid % ROW_DEV
    run = local // run_rows
    peer = (owner + run) % N_ROWS
    block = owner * N_ROWS + run
    pick = (local % run_rows)[:, None] * STENCIL + jnp.arange(STENCIL, dtype=jnp.int32)[None, :]
    scores = jax.random.randint(k1, (N_ROWS * N_ROWS, CAP), 0, 1048576, dtype=jnp.int32) * CAP + jnp.arange(CAP, dtype=jnp.int32)[None, :]
    ranking = jnp.argsort(scores, axis=1, stable=True).astype(jnp.int32)
    covered = ranking[block[:, None], jnp.minimum(pick, CAP - 1)]
    spare = jax.random.randint(k2, (ROWS, STENCIL), 0, CAP, dtype=jnp.int32)
    column = jnp.where(pick < CAP, covered, spare)
    return (peer[:, None] * CAP + column).astype(jnp.int32)


def touch_ends(array, own_key, smallest, largest):
    place = [jax.random.randint(jax.random.fold_in(own_key, axis), (), 0, length) for axis, length in enumerate(array.shape)]
    longest = array.shape.index(max(array.shape))
    neighbour = place[:longest] + [(place[longest] + 1) % array.shape[longest]] + place[longest + 1:]
    return array.at[tuple(place)].set(smallest).at[tuple(neighbour)].set(largest)


def levels(rng, dims, cuts, low, high):
    level = 1.0
    for axis_at, shards_of in cuts:
        steps = jax.random.uniform(jax.random.fold_in(jax.random.fold_in(rng, 6), axis_at), (shards_of,), jnp.float32, low / len(cuts), high / len(cuts))
        level = level * jnp.repeat(jnp.exp(steps), dims[axis_at] // shards_of).reshape((-1,) + (1,) * (len(dims) - 1 - axis_at))
    return level


def setup_inputs(seed: int = 0) -> dict:
    streams_of = jax.random.split(jax.random.key(seed), 5)
    return {
        "snapshots": draw_snapshots(jax.random.fold_in(streams_of[4], 71), 0),
        "send_list": touch_ends(jax.random.randint(streams_of[1], (N_ROWS * N_ROWS, CAP), 0, NODE_DEV), jax.random.fold_in(streams_of[1], 1), 0, NODE_DEV - 1).astype(jnp.int32),
        "stencil": draw_stencil(jax.random.fold_in(streams_of[4], 71), 0),
        "weights": jnp.clip(0.2 + 0.8 * jax.random.uniform(streams_of[3], (ROWS, STENCIL), jnp.float32) ** levels(streams_of[3], (ROWS, STENCIL), ((0, 32),), -0.2, 0.2), 0.2, 1.0),
    }


def reference(snapshots, send_list, stencil, weights):
    rowid = jnp.arange(ROWS, dtype=jnp.int32)
    owner = rowid // ROW_DEV
    field = jnp.zeros((ROWS, SNAPS), jnp.float32)
    for s in range(STENCIL):
        slot = stencil[:, s]
        peer = slot // CAP
        col = slot % CAP
        node = send_list[peer * N_ROWS + owner, col]
        gidx = (peer * NODE_DEV + node).astype(jnp.int32)
        field = field + weights[:, s][:, None] * snapshots[gidx]
    qmat, rmat = jnp.linalg.qr(field)
    signs = jnp.sign(jnp.diagonal(rmat))
    qmat = qmat * signs[None, :]
    rmat = rmat * signs[:, None]
    scale = jnp.sqrt(jnp.float32(ROWS))
    return (qmat * scale, rmat / scale)
```

```python
import functools
import math

import jax
import jax.numpy as jnp
from jax import lax
from jax.experimental import pallas as pl
from jax.experimental.pallas import tpu as pltpu
from jax.sharding import PartitionSpec as P

F32 = jnp.float32
BF16 = jnp.bfloat16
TILE = 8
VMEM_LIMIT = 56 * 1024 * 1024


def exact(left, right, dims=((1,), (0,))):
    return lax.dot_general(left, right, (dims, ((), ())), precision=lax.Precision.HIGHEST, preferred_element_type=F32)


def rough(left, right, dims=((1,), (0,))):
    return lax.dot_general(left.astype(BF16), right.astype(BF16), (dims, ((), ())), preferred_element_type=F32)


def pick_kernel(send_ref, snap_ref, out_ref):
    peers, cap = send_ref.shape

    def one_peer(peer, carry):
        base = peer * cap
        for slot in range(cap):
            node = send_ref[peer, slot]
            out_ref[pl.ds(base + slot, 1), :] = snap_ref[pl.ds(node, 1), :]
        return carry

    lax.fori_loop(0, peers, one_peer, 0)


def pick_donors(snapshots, send_list):
    peers, cap = send_list.shape
    return pl.pallas_call(
        pick_kernel,
        out_shape=jax.ShapeDtypeStruct((peers * cap, snapshots.shape[1]), F32),
        in_specs=[pl.BlockSpec(memory_space=pltpu.SMEM), pl.BlockSpec(memory_space=pltpu.VMEM)],
        out_specs=pl.BlockSpec(memory_space=pltpu.VMEM),
        compiler_params=pltpu.CompilerParams(vmem_limit_bytes=VMEM_LIMIT),
        name="pick_donors",
    )(send_list, snapshots)


def weave_kernel(runs, run_rows, cap, peers, me_ref, sten_ref, wt_ref, mat_ref, slot_ref):
    step = pl.program_id(0)
    iota = lax.broadcasted_iota(jnp.int32, (cap, run_rows), 0)
    for sub in range(runs):
        run = step * runs + sub
        peer = lax.rem(me_ref[0] + run, peers)
        cols = slice(sub * run_rows, (sub + 1) * run_rows)
        dense = jnp.zeros((cap, run_rows), F32)
        for s in range(sten_ref.shape[0]):
            place = jnp.broadcast_to(sten_ref[s : s + 1, cols] - peer * cap, (cap, run_rows))
            value = jnp.broadcast_to(wt_ref[s : s + 1, cols], (cap, run_rows))
            dense = dense + jnp.where(iota == place, value, 0.0)
        high = dense.astype(BF16)
        high_f = high.astype(F32)
        low_f = (dense - high_f).astype(BF16).astype(F32)
        pair = jnp.concatenate([high_f, low_f], axis=0)
        mat = pair.T.astype(BF16)
        mat_ref[cols, :] = mat
        gram = jnp.dot(pair.astype(BF16), mat, preferred_element_type=F32)
        half = gram[:cap] + gram[cap:]
        slot_ref[sub * cap : (sub + 1) * cap, :] = half[:, :cap] + half[:, cap:]


def weave(me, stencil, weights, peers, cap):
    rows = stencil.shape[0]
    run_rows = rows // peers
    runs = max(1, 2048 // run_rows)
    block = runs * run_rows
    grid_spec = pltpu.PrefetchScalarGridSpec(
        num_scalar_prefetch=1,
        grid=(peers // runs,),
        in_specs=[
            pl.BlockSpec((stencil.shape[1], block), lambda i, m: (0, i)),
            pl.BlockSpec((stencil.shape[1], block), lambda i, m: (0, i)),
        ],
        out_specs=[
            pl.BlockSpec((block, 2 * cap), lambda i, m: (i, 0)),
            pl.BlockSpec((runs * cap, cap), lambda i, m: (i, 0)),
        ],
    )
    return pl.pallas_call(
        functools.partial(weave_kernel, runs, run_rows, cap, peers),
        out_shape=[jax.ShapeDtypeStruct((rows, 2 * cap), BF16), jax.ShapeDtypeStruct((peers * cap, cap), F32)],
        grid_spec=grid_spec,
        compiler_params=pltpu.CompilerParams(vmem_limit_bytes=VMEM_LIMIT),
        cost_estimate=pl.CostEstimate(flops=8 * 10**9, bytes_accessed=40 * 10**6, transcendentals=0),
        name="weave",
    )(me, stencil.T, weights.T)


def two_sum(a, b):
    s = a + b
    t = s - a
    return s, (a - (s - t)) + (b - t)


def merge(a, b):
    s, e = two_sum(a[0], b[0])
    low = (a[1] + b[1]) + e
    high = s + low
    return high, low - (high - s)


def gram_kernel(peers, cap, me_ref, x_ref, slot_ref, keep_ref, give_ref, z_ref):
    snaps = x_ref.shape[1]

    def one_run(run, carry):
        peer = lax.rem(me_ref[0] + run, peers)
        at = pl.ds(pl.multiple_of(peer * cap, cap), cap)
        frm = pl.ds(pl.multiple_of(run * cap, cap), cap)
        z_ref[at, :] = exact(slot_ref[frm, :], x_ref[at, :])
        return carry

    lax.fori_loop(0, peers, one_run, 0, unroll=4)
    chunk = 256

    def one_chunk(i, carry):
        at = pl.ds(pl.multiple_of(i * chunk, chunk), chunk)
        part = exact(x_ref[at, :], z_ref[at, :], ((0,), (0,)))
        s, e = two_sum(carry[0], part)
        return s, carry[1] + e

    zero = jnp.zeros((snaps, snaps), F32)
    high, low = lax.fori_loop(0, peers * cap // chunk, one_chunk, (zero, zero), unroll=2)
    half = snaps // 2
    core = lax.rem(me_ref[0], 2)
    for ref, want in ((keep_ref, 0), (give_ref, 1)):
        for i, part in enumerate((high, low)):
            ref[i] = jnp.where(core == want, part[:half], part[half:])


def local_gram(me, x, slots, peers, cap):
    snaps = x.shape[1]
    shape = jax.ShapeDtypeStruct((2, snaps // 2, snaps), F32)
    vmem = pl.BlockSpec(memory_space=pltpu.VMEM)
    return pl.pallas_call(
        functools.partial(gram_kernel, peers, cap),
        out_shape=[shape, shape],
        in_specs=[pl.BlockSpec(memory_space=pltpu.SMEM), vmem, vmem],
        out_specs=[vmem, vmem],
        scratch_shapes=[pltpu.VMEM(x.shape, F32)],
        compiler_params=pltpu.CompilerParams(vmem_limit_bytes=VMEM_LIMIT),
        name="local_gram",
    )(me, x, slots)


def hop(value, mask, peers):
    return lax.ppermute(value, "rows", [(i, i ^ mask) for i in range(peers)])


def sum_pairs(keep, give, peers):
    other = hop(give, 1, peers)
    mine = merge((keep[0], keep[1]), (other[0], other[1]))
    bit = 2
    while bit < peers:
        now = jnp.stack(mine)
        if bit * 2 < peers:
            a = hop(now, bit, peers)
            b = hop(now, 2 * bit, peers)
            c = hop(now, 3 * bit, peers)
            mine = merge(merge(mine, (a[0], a[1])), merge((b[0], b[1]), (c[0], c[1])))
            bit *= 4
        else:
            a = hop(now, bit, peers)
            mine = merge(mine, (a[0], a[1]))
            bit *= 2
    now = jnp.stack(mine)
    return now, hop(now, 1, peers)


def power_scale(value):
    scale = jnp.ones_like(value)
    for k in (32, 16, 8, 4, 2, 1):
        small = value < 2.0 ** (2 - 2 * k)
        value = jnp.where(small, value * 2.0 ** (2 * k), value)
        scale = jnp.where(small, scale * 2.0**k, scale)
    for k in (32, 16, 8, 4, 2, 1):
        large = value >= 2.0 ** (2 * k)
        value = jnp.where(large, value * 2.0 ** (-2 * k), value)
        scale = jnp.where(large, scale * 2.0**-k, scale)
    return scale


def factor(gram):
    size = gram.shape[0]
    sub = lax.broadcasted_iota(jnp.int32, (TILE, size), 0)
    lane = lax.broadcasted_iota(jnp.int32, (TILE, size), 1)
    left = gram
    right = (lax.broadcasted_iota(jnp.int32, (size, size), 0) == lax.broadcasted_iota(jnp.int32, (size, size), 1)).astype(F32)
    tops, inverses = [], []
    for j in range(size // TILE):
        head, tail = left[:TILE], left[TILE:]
        ihead, itail = right[:TILE], right[TILE:]
        pivots = jnp.ones((TILE, size), F32)
        for k in range(TILE):
            col = j * TILE + k
            row = jnp.broadcast_to(head[k : k + 1, :], (TILE, size))
            irow = jnp.broadcast_to(ihead[k : k + 1, :], (TILE, size))
            pivot = jnp.broadcast_to(row[:, col : col + 1], (TILE, size))
            pivots = jnp.where(sub == k, pivot, pivots)
            over = 1.0 / pivot
            row = row * over
            irow = irow * over
            coef = jnp.where(sub > k, jnp.broadcast_to(head[:, col : col + 1], (TILE, size)), 0.0)
            head = head - coef * row
            ihead = ihead - coef * irow
            rest = tail.shape[0]
            if rest:
                coef = jnp.broadcast_to(tail[:, col : col + 1], (rest, size))
                many = rest // TILE
                tail = tail - coef * jnp.concatenate([row] * many, axis=0)
                itail = itail - coef * jnp.concatenate([irow] * many, axis=0)
        root = lax.rsqrt(pivots)
        tops.append(jnp.where(lane >= sub + j * TILE, head * root, 0.0))
        inverses.append(ihead * root)
        left, right = tail, itail
    return jnp.concatenate(tops, axis=0), jnp.concatenate(inverses, axis=0)


def slices(value):
    out = []
    for bits in (6, 14, 22, 30):
        big = 1.5 * 2.0 ** (23 - bits)
        piece = (value + big) - big
        value = value - piece
        out.append(piece.astype(BF16))
    return out


def triangular(high, low):
    size = high.shape[0]
    rows = lax.broadcasted_iota(jnp.int32, (size, size), 0)
    cols = lax.broadcasted_iota(jnp.int32, (size, size), 1)
    diagonal = jnp.where(rows == cols, high, 0.0)
    across = power_scale(jnp.sum(diagonal, axis=0, keepdims=True))
    down = power_scale(jnp.sum(diagonal, axis=1, keepdims=True))
    high = high * across * down
    low = low * across * down
    upper, inv_t = factor(high)
    up = slices(upper)
    lo = slices(upper.T)
    first = jnp.dot(lo[0], jnp.concatenate(up, axis=1), preferred_element_type=F32)
    second = jnp.dot(lo[1], jnp.concatenate(up[:3], axis=1), preferred_element_type=F32)
    third = jnp.dot(lo[2], jnp.concatenate(up[:2], axis=1), preferred_element_type=F32)
    fourth = jnp.dot(lo[3], up[0], preferred_element_type=F32)
    rest = high - first[:, :size]
    rest = rest - (first[:, size : 2 * size] + second[:, :size])
    rest = rest - second[:, size : 2 * size]
    rest = rest - (first[:, 2 * size : 3 * size] + third[:, :size])
    rest = rest + low
    rest = rest - ((first[:, 3 * size :] + fourth) + (second[:, 2 * size :] + third[:, size:]))
    inv = inv_t.T
    error = exact(exact(inv_t, rest), inv)
    weight = jnp.where(rows < cols, 1.0, jnp.where(rows == cols, 0.5, 0.0))
    shift = error * weight
    for _ in range(2):
        shift = (error - rough(shift, shift, ((0,), (0,)))) * weight
    square = rough(shift, shift)
    minus = square - shift
    minus = minus + rough(square, minus)
    inv = inv + exact(inv, minus)
    upper = upper + exact(shift, upper)
    return upper * (1.0 / across), inv * down


def basis_kernel(runs, run_rows, cap, peers, scale, me_ref, mine_ref, other_ref, x_ref, mat_ref, out_ref, r_ref, inv_ref):
    step = pl.program_id(0)

    @pl.when(step == 0)
    def _():
        core = lax.rem(me_ref[0], 2)
        parts = []
        for i in range(2):
            mine, other = mine_ref[i], other_ref[i]
            top = jnp.where(core == 0, mine, other)
            low = jnp.where(core == 0, other, mine)
            parts.append(jnp.concatenate([top, low], axis=0))
        upper, inv = triangular(parts[0], parts[1])
        r_ref[...] = upper * (1.0 / scale)
        inv_ref[...] = inv * scale

    for sub in range(runs):
        peer = lax.rem(me_ref[0] + step * runs + sub, peers)
        at = pl.ds(pl.multiple_of(peer * cap, cap), cap)
        y = exact(x_ref[at, :], inv_ref[...])
        high = y.astype(BF16)
        low = (y - high.astype(F32)).astype(BF16)
        both = jnp.concatenate([high, low], axis=1)
        both = jnp.concatenate([both, both], axis=0)
        rows = slice(sub * run_rows, (sub + 1) * run_rows)
        twice = jnp.dot(mat_ref[rows, :], both, preferred_element_type=F32)
        snaps = y.shape[1]
        out_ref[rows, :] = twice[:, :snaps] + twice[:, snaps:]


def make_basis(me, mine, other, x, mat, peers, cap, total_rows):
    rows = mat.shape[0]
    snaps = x.shape[1]
    run_rows = rows // peers
    runs = max(1, 1024 // run_rows)
    block = runs * run_rows
    whole = lambda *dims: pl.BlockSpec(dims, lambda i, m: (0,) * len(dims))
    grid_spec = pltpu.PrefetchScalarGridSpec(
        num_scalar_prefetch=1,
        grid=(peers // runs,),
        in_specs=[whole(*mine.shape), whole(*other.shape), whole(*x.shape), pl.BlockSpec((block, 2 * cap), lambda i, m: (i, 0))],
        out_specs=[pl.BlockSpec((block, snaps), lambda i, m: (i, 0)), whole(snaps, snaps)],
        scratch_shapes=[pltpu.VMEM((snaps, snaps), F32)],
    )
    return pl.pallas_call(
        functools.partial(basis_kernel, runs, run_rows, cap, peers, math.sqrt(total_rows)),
        out_shape=[jax.ShapeDtypeStruct((rows, snaps), F32), jax.ShapeDtypeStruct((snaps, snaps), F32)],
        grid_spec=grid_spec,
        compiler_params=pltpu.CompilerParams(vmem_limit_bytes=VMEM_LIMIT),
        name="make_basis",
    )(me, mine, other, x, mat)


def body(snapshots, send_list, stencil, weights):
    peers, cap = send_list.shape
    total_rows = stencil.shape[0] * peers
    me = lax.axis_index("rows").astype(jnp.int32).reshape(1)
    outgoing = pick_donors(snapshots, send_list)
    x = lax.all_to_all(outgoing, "rows", split_axis=0, concat_axis=0, tiled=True)
    mat, slots = weave(me, stencil, weights, peers, cap)
    keep, give = local_gram(me, x, slots, peers, cap)
    mine, other = sum_pairs(keep, give, peers)
    basis, r_factor = make_basis(me, mine, other, x, mat, peers, cap, total_rows)
    return (basis, r_factor)


def solution(mesh):
    return jax.shard_map(
        body,
        mesh=mesh,
        in_specs=(P("rows", None), P("rows", None), P("rows", None), P("rows", None)),
        out_specs=(P("rows", None), P()),
        check_vma=False,
    )
```

```python
import functools
import math

import jax
import jax.numpy as jnp
from jax import lax
from jax.experimental import pallas as pl
from jax.experimental.pallas import tpu as pltpu
from jax.sharding import PartitionSpec as P

F32 = jnp.float32
BF16 = jnp.bfloat16
TILE = 8


def exact(left, right, dims=((1,), (0,))):
    return lax.dot_general(left, right, (dims, ((), ())), precision=lax.Precision.HIGHEST, preferred_element_type=F32)


def rough(left, right, dims=((1,), (0,))):
    return lax.dot_general(left.astype(BF16), right.astype(BF16), (dims, ((), ())), preferred_element_type=F32)


PIECES = 8
MOST_VMEM = 60 * 1024 * 1024


def limit(*arrays):
    total = 0
    for shape, dtype in arrays:
        lanes = -(-shape[-1] // 128) * 128
        total += math.prod(shape[:-1]) * lanes * jnp.dtype(dtype).itemsize
    return total + 8 * 1024 * 1024


def pick_kernel(send_ref, snap_ref, out_ref, held_ref, sems):
    peers, cap = send_ref.shape
    part = snap_ref.shape[0] // PIECES
    copies = []
    for i in range(PIECES):
        at = pl.ds(i * part, part)
        copy = pltpu.make_async_copy(snap_ref.at[at, :], held_ref.at[at, :], sems.at[i])
        copy.start()
        copies.append(copy)
    for copy in copies:
        copy.wait()

    def one_peer(peer, carry):
        base = peer * cap
        for slot in range(cap):
            node = send_ref[peer, slot]
            out_ref[pl.ds(base + slot, 1), :] = held_ref[pl.ds(node, 1), :]
        return carry

    lax.fori_loop(0, peers, one_peer, 0)


def pick_donors(snapshots, send_list):
    peers, cap = send_list.shape
    snaps = snapshots.shape[1]
    return pl.pallas_call(
        pick_kernel,
        out_shape=jax.ShapeDtypeStruct((peers * cap, snaps), F32),
        in_specs=[pl.BlockSpec(memory_space=pltpu.SMEM), pl.BlockSpec(memory_space=pltpu.HBM)],
        out_specs=pl.BlockSpec(memory_space=pltpu.VMEM),
        scratch_shapes=[pltpu.VMEM(snapshots.shape, F32), pltpu.SemaphoreType.DMA((PIECES,))],
        compiler_params=pltpu.CompilerParams(vmem_limit_bytes=MOST_VMEM),
        name="pick_donors",
    )(send_list, snapshots)


def weave_kernel(runs, run_rows, cap, peers, me_ref, sten_ref, wt_ref, mat_ref, slot_ref):
    step = pl.program_id(0)
    iota = lax.broadcasted_iota(jnp.int32, (cap, run_rows), 0)
    for sub in range(runs):
        run = step * runs + sub
        peer = lax.rem(me_ref[0] + run, peers)
        cols = slice(sub * run_rows, (sub + 1) * run_rows)
        dense = jnp.zeros((cap, run_rows), F32)
        for s in range(sten_ref.shape[0]):
            place = jnp.broadcast_to(sten_ref[s : s + 1, cols] - peer * cap, (cap, run_rows))
            value = jnp.broadcast_to(wt_ref[s : s + 1, cols], (cap, run_rows))
            dense = dense + jnp.where(iota == place, value, 0.0)
        high = dense.astype(BF16)
        high_f = high.astype(F32)
        low_f = (dense - high_f).astype(BF16).astype(F32)
        pair = jnp.concatenate([high_f, low_f], axis=0)
        mat = pair.T.astype(BF16)
        mat_ref[cols, :] = mat
        gram = jnp.dot(pair.astype(BF16), mat, preferred_element_type=F32)
        half = gram[:cap] + gram[cap:]
        slot_ref[sub * cap : (sub + 1) * cap, :] = half[:, :cap] + half[:, cap:]


def weave(me, stencil, weights, peers, cap):
    rows = stencil.shape[0]
    run_rows = rows // peers
    runs = max(1, 2048 // run_rows)
    block = runs * run_rows
    grid_spec = pltpu.PrefetchScalarGridSpec(
        num_scalar_prefetch=1,
        grid=(peers // runs,),
        in_specs=[
            pl.BlockSpec((stencil.shape[1], block), lambda i, m: (0, i)),
            pl.BlockSpec((stencil.shape[1], block), lambda i, m: (0, i)),
        ],
        out_specs=[
            pl.BlockSpec((block, 2 * cap), lambda i, m: (i, 0)),
            pl.BlockSpec((runs * cap, cap), lambda i, m: (i, 0)),
        ],
    )
    return pl.pallas_call(
        functools.partial(weave_kernel, runs, run_rows, cap, peers),
        out_shape=[jax.ShapeDtypeStruct((rows, 2 * cap), BF16), jax.ShapeDtypeStruct((peers * cap, cap), F32)],
        grid_spec=grid_spec,
        compiler_params=pltpu.CompilerParams(vmem_limit_bytes=16 * 1024 * 1024),
        cost_estimate=pl.CostEstimate(flops=8 * 10**9, bytes_accessed=40 * 10**6, transcendentals=0),
        name="weave",
    )(me, stencil.T, weights.T)


def two_sum(a, b):
    s = a + b
    t = s - a
    return s, (a - (s - t)) + (b - t)


def merge(a, b):
    s, e = two_sum(a[0], b[0])
    low = (a[1] + b[1]) + e
    high = s + low
    return high, low - (high - s)


def gram_kernel(peers, cap, me_ref, x_ref, slot_ref, keep_ref, give_ref, z_ref):
    snaps = x_ref.shape[1]

    def one_run(run, carry):
        peer = lax.rem(me_ref[0] + run, peers)
        at = pl.ds(pl.multiple_of(peer * cap, cap), cap)
        frm = pl.ds(pl.multiple_of(run * cap, cap), cap)
        z_ref[at, :] = exact(slot_ref[frm, :], x_ref[at, :])
        return carry

    lax.fori_loop(0, peers, one_run, 0, unroll=16)
    chunk = 256

    def one_chunk(i, carry):
        at = pl.ds(pl.multiple_of(i * chunk, chunk), chunk)
        part = exact(x_ref[at, :], z_ref[at, :], ((0,), (0,)))
        s, e = two_sum(carry[0], part)
        return s, carry[1] + e

    zero = jnp.zeros((snaps, snaps), F32)
    high, low = lax.fori_loop(0, peers * cap // chunk, one_chunk, (zero, zero), unroll=8)
    half = snaps // 2
    core = lax.rem(me_ref[0], 2)
    for ref, want in ((keep_ref, 0), (give_ref, 1)):
        for i, part in enumerate((high, low)):
            ref[i] = jnp.where(core == want, part[:half], part[half:])


def local_gram(me, x, slots, peers, cap):
    snaps = x.shape[1]
    shape = jax.ShapeDtypeStruct((2, snaps // 2, snaps), F32)
    vmem = pl.BlockSpec(memory_space=pltpu.VMEM)
    return pl.pallas_call(
        functools.partial(gram_kernel, peers, cap),
        out_shape=[shape, shape],
        in_specs=[pl.BlockSpec(memory_space=pltpu.SMEM), vmem, vmem],
        out_specs=[vmem, vmem],
        scratch_shapes=[pltpu.VMEM(x.shape, F32)],
        compiler_params=pltpu.CompilerParams(vmem_limit_bytes=limit((x.shape, F32), (x.shape, F32), (slots.shape, F32))),
        name="local_gram",
    )(me, x, slots)


def hop(value, mask, peers):
    return lax.ppermute(value, "rows", [(i, i ^ mask) for i in range(peers)])


def sum_pairs(keep, give, peers):
    other = hop(give, 1, peers)
    mine = merge((keep[0], keep[1]), (other[0], other[1]))
    bit = 2
    while bit < peers:
        now = jnp.stack(mine)
        if bit * 2 < peers:
            a = hop(now, bit, peers)
            b = hop(now, 2 * bit, peers)
            c = hop(now, 3 * bit, peers)
            mine = merge(merge(mine, (a[0], a[1])), merge((b[0], b[1]), (c[0], c[1])))
            bit *= 4
        else:
            a = hop(now, bit, peers)
            mine = merge(mine, (a[0], a[1]))
            bit *= 2
    now = jnp.stack(mine)
    return now, hop(now, 1, peers)


def power_scale(value):
    scale = jnp.ones_like(value)
    for k in (32, 16, 8, 4, 2, 1):
        small = value < 2.0 ** (2 - 2 * k)
        value = jnp.where(small, value * 2.0 ** (2 * k), value)
        scale = jnp.where(small, scale * 2.0**k, scale)
    for k in (32, 16, 8, 4, 2, 1):
        large = value >= 2.0 ** (2 * k)
        value = jnp.where(large, value * 2.0 ** (-2 * k), value)
        scale = jnp.where(large, scale * 2.0**-k, scale)
    return scale


def factor(gram):
    size = gram.shape[0]
    tile = (TILE, size)
    sub = lax.broadcasted_iota(jnp.int32, tile, 0)
    lane = lax.broadcasted_iota(jnp.int32, tile, 1)
    left = gram
    right = (lax.broadcasted_iota(jnp.int32, (size, size), 0) == lax.broadcasted_iota(jnp.int32, (size, size), 1)).astype(F32)
    tops, inverses = [], []
    for j in range(size // TILE):
        rest = left.shape[0] - TILE
        many = rest // TILE
        columns = [left[:, j * TILE + k : j * TILE + k + 1] for k in range(TILE)]
        heads = [jnp.broadcast_to(column[:TILE], tile) for column in columns]
        tails = [jnp.broadcast_to(column[TILE:], (rest, size)) for column in columns] if rest else []
        block = [[jnp.broadcast_to(heads[k][i : i + 1, :], tile) for k in range(i + 1)] for i in range(TILE)]
        rows = [jnp.broadcast_to(left[k : k + 1, :], tile) for k in range(TILE)]
        irows = [jnp.broadcast_to(right[k : k + 1, :], tile) for k in range(TILE)]
        over, coef = [], {}
        for k in range(TILE):
            over.append(1.0 / block[k][k])
            for i in range(k + 1, TILE):
                coef[i, k] = block[i][k] * over[k]
                for c in range(k + 1, i + 1):
                    block[i][c] = block[i][c] - (block[i][k] * block[c][k]) * over[k]
                rows[i] = rows[i] - coef[i, k] * rows[k]
                irows[i] = irows[i] - coef[i, k] * irows[k]
        top, inverse, pivots = rows[0], irows[0], block[0][0]
        for k in range(1, TILE):
            top = jnp.where(sub == k, rows[k], top)
            inverse = jnp.where(sub == k, irows[k], inverse)
            pivots = jnp.where(sub == k, block[k][k], pivots)
        root = lax.rsqrt(pivots)
        tops.append(jnp.where(lane >= sub + j * TILE, top * root, 0.0))
        inverses.append(inverse * root)
        if rest:
            solved = [rows[k] * over[k] for k in range(TILE)]
            isolved = [irows[k] * over[k] for k in range(TILE)]
            for k in reversed(range(TILE)):
                for i in range(k):
                    solved[i] = solved[i] - coef[k, i] * solved[k]
                    isolved[i] = isolved[i] - coef[k, i] * isolved[k]
            left, right = left[TILE:], right[TILE:]
            for k in range(TILE):
                left = left - tails[k] * jnp.concatenate([solved[k]] * many, axis=0)
                right = right - tails[k] * jnp.concatenate([isolved[k]] * many, axis=0)
    return jnp.concatenate(tops, axis=0), jnp.concatenate(inverses, axis=0)


def slices(value):
    out = []
    for bits in (6, 14, 22, 30):
        big = 1.5 * 2.0 ** (23 - bits)
        piece = (value + big) - big
        value = value - piece
        out.append(piece.astype(BF16))
    return out


def triangular(high, low):
    size = high.shape[0]
    rows = lax.broadcasted_iota(jnp.int32, (size, size), 0)
    cols = lax.broadcasted_iota(jnp.int32, (size, size), 1)
    diagonal = jnp.where(rows == cols, high, 0.0)
    across = power_scale(jnp.sum(diagonal, axis=0, keepdims=True))
    down = power_scale(jnp.sum(diagonal, axis=1, keepdims=True))
    high = high * across * down
    low = low * across * down
    upper, inv_t = factor(high)
    up = slices(upper)
    lo = slices(upper.T)
    first = jnp.dot(lo[0], jnp.concatenate(up, axis=1), preferred_element_type=F32)
    second = jnp.dot(lo[1], jnp.concatenate(up[:3], axis=1), preferred_element_type=F32)
    third = jnp.dot(lo[2], jnp.concatenate(up[:2], axis=1), preferred_element_type=F32)
    fourth = jnp.dot(lo[3], up[0], preferred_element_type=F32)
    rest = high - first[:, :size]
    rest = rest - (first[:, size : 2 * size] + second[:, :size])
    rest = rest - second[:, size : 2 * size]
    rest = rest - (first[:, 2 * size : 3 * size] + third[:, :size])
    rest = rest + low
    rest = rest - ((first[:, 3 * size :] + fourth) + (second[:, 2 * size :] + third[:, size:]))
    inv = inv_t.T
    slip = jnp.where(rows <= cols, exact(upper, inv) - (rows == cols).astype(F32), 0.0)
    weight = jnp.where(rows < cols, 1.0, jnp.where(rows == cols, 0.5, 0.0))
    error = exact(exact(inv_t, rest), inv) + rough(slip, slip, ((0,), (0,)))
    shift = error * weight + slip
    for _ in range(2):
        shift = (error - rough(shift, shift, ((0,), (0,)))) * weight + slip
    square = rough(shift, shift)
    minus = square - shift
    minus = minus + rough(square, minus)
    inv = inv + exact(inv, minus)
    upper = upper + exact(shift - slip - rough(shift, slip), upper)
    return upper * (1.0 / across), inv * down


def thirds(value):
    high = value.astype(BF16)
    rest = value - high.astype(F32)
    middle = rest.astype(BF16)
    return high, middle, (rest - middle.astype(F32)).astype(BF16)


CHUNKS = 16


def basis_kernel(
    cap, peers, scale, me_ref, mine_ref, other_ref, x_ref, mat_hbm, out_hbm, r_ref, y_ref, mat_ref, out_ref, sems, in_sem
):
    slots, snaps = x_ref.shape
    fetch = pltpu.make_async_copy(mat_hbm, mat_ref, in_sem)
    fetch.start()
    core = lax.rem(me_ref[0], 2)
    parts = []
    for i in range(2):
        mine, other = mine_ref[i], other_ref[i]
        top = jnp.where(core == 0, mine, other)
        low = jnp.where(core == 0, other, mine)
        parts.append(jnp.concatenate([top, low], axis=0))
    upper, inv = triangular(parts[0], parts[1])
    r_ref[...] = upper * (1.0 / scale)
    high, middle, low = thirds(inv * scale)
    wide = jnp.concatenate([high, middle], axis=1)
    wide = jnp.concatenate([wide, wide], axis=0)
    tall = jnp.concatenate([low, high], axis=0)
    chunk = 512

    def one_chunk(i, carry):
        at = pl.ds(pl.multiple_of(i * chunk, chunk), chunk)
        high, middle, low = thirds(x_ref[at, :])
        first = jnp.dot(jnp.concatenate([high, middle], axis=1), wide, preferred_element_type=F32)
        second = jnp.dot(jnp.concatenate([high, low], axis=1), tall, preferred_element_type=F32)
        y = first[:, :snaps] + (first[:, snaps:] + second)
        y_high = y.astype(BF16)
        y_ref[at, :snaps] = y_high
        y_ref[at, snaps:] = (y - y_high.astype(F32)).astype(BF16)
        return carry

    lax.fori_loop(0, slots // chunk, one_chunk, 0)
    fetch.wait()
    rows = mat_ref.shape[0]
    block = rows // CHUNKS
    run_rows = rows // peers
    runs = block // run_rows

    def send(i):
        at = pl.ds(pl.multiple_of(i * block, block), block)
        return pltpu.make_async_copy(out_ref.at[at, :], out_hbm.at[at, :], sems.at[i])

    def one_block(i, carry):
        for sub in range(runs):
            run = i * runs + sub
            peer = lax.rem(me_ref[0] + run, peers)
            both = y_ref[pl.ds(pl.multiple_of(peer * cap, cap), cap), :]
            both = jnp.concatenate([both, both], axis=0)
            at = pl.ds(pl.multiple_of(run * run_rows, run_rows), run_rows)
            twice = jnp.dot(mat_ref[at, :], both, preferred_element_type=F32)
            out_ref[at, :] = twice[:, :snaps] + twice[:, snaps:]
        send(i).start()
        return carry

    lax.fori_loop(0, CHUNKS, one_block, 0)

    def one_wait(i, carry):
        send(i).wait()
        return carry

    lax.fori_loop(0, CHUNKS, one_wait, 0)


def make_basis(me, mine, other, x, mat, peers, cap, total_rows):
    rows = mat.shape[0]
    slots, snaps = x.shape
    vmem = pl.BlockSpec(memory_space=pltpu.VMEM)
    hbm = pl.BlockSpec(memory_space=pltpu.HBM)
    held = [((slots, 2 * snaps), BF16), (mat.shape, BF16), ((rows, snaps), F32)]
    return pl.pallas_call(
        functools.partial(basis_kernel, cap, peers, math.sqrt(total_rows)),
        out_shape=[jax.ShapeDtypeStruct((rows, snaps), F32), jax.ShapeDtypeStruct((snaps, snaps), F32)],
        in_specs=[pl.BlockSpec(memory_space=pltpu.SMEM), vmem, vmem, vmem, hbm],
        out_specs=[hbm, vmem],
        scratch_shapes=[pltpu.VMEM(*h) for h in held] + [pltpu.SemaphoreType.DMA((CHUNKS,)), pltpu.SemaphoreType.DMA(())],
        compiler_params=pltpu.CompilerParams(vmem_limit_bytes=MOST_VMEM),
        name="make_basis",
    )(me, mine, other, x, mat)


def body(snapshots, send_list, stencil, weights):
    peers, cap = send_list.shape
    total_rows = stencil.shape[0] * peers
    me = lax.axis_index("rows").astype(jnp.int32).reshape(1)
    outgoing = pick_donors(snapshots, send_list)
    x = lax.all_to_all(outgoing, "rows", split_axis=0, concat_axis=0, tiled=True)
    mat, slots = weave(me, stencil, weights, peers, cap)
    keep, give = local_gram(me, x, slots, peers, cap)
    mine, other = sum_pairs(keep, give, peers)
    basis, r_factor = make_basis(me, mine, other, x, mat, peers, cap, total_rows)
    return (basis, r_factor)


def solution(mesh):
    return jax.shard_map(
        body,
        mesh=mesh,
        in_specs=(P("rows", None), P("rows", None), P("rows", None), P("rows", None)),
        out_specs=(P("rows", None), P()),
        check_vma=False,
    )
```

```python
import functools
import math

import jax
import jax.numpy as jnp
from jax import lax
from jax.experimental import pallas as pl
from jax.experimental.pallas import tpu as pltpu
from jax.sharding import PartitionSpec as P

F32 = jnp.float32
BF16 = jnp.bfloat16
TILE = 8


def exact(left, right, dims=((1,), (0,))):
    return lax.dot_general(left, right, (dims, ((), ())), precision=lax.Precision.HIGHEST, preferred_element_type=F32)


def rough(left, right, dims=((1,), (0,))):
    return lax.dot_general(left.astype(BF16), right.astype(BF16), (dims, ((), ())), preferred_element_type=F32)


PIECES = 8
GROUPS = 4
MOST_VMEM = 58 * 1024 * 1024
BASIS_VMEM = 50 * 1024 * 1024


def limit(*arrays):
    total = 0
    for shape, dtype in arrays:
        lanes = -(-shape[-1] // 128) * 128
        total += math.prod(shape[:-1]) * lanes * jnp.dtype(dtype).itemsize
    return total + 8 * 1024 * 1024


def pick_kernel(send_hbm, snap_hbm, out_hbm, held_ref, out_ref, send_ref, sems, out_sems, list_sem):
    peers, cap = send_hbm.shape
    part = snap_hbm.shape[0] // PIECES
    listed = pltpu.make_async_copy(send_hbm, send_ref, list_sem)
    listed.start()
    copies = []
    for i in range(PIECES):
        at = pl.ds(i * part, part)
        copy = pltpu.make_async_copy(snap_hbm.at[at, :], held_ref.at[at, :], sems.at[i])
        copy.start()
        copies.append(copy)
    listed.wait()
    for copy in copies:
        copy.wait()
    group = peers // GROUPS

    def one_peer(peer, carry):
        base = peer * cap
        for slot in range(cap):
            node = send_ref[peer, slot]
            out_ref[pl.ds(base + slot, 1), :] = held_ref[pl.ds(node, 1), :]
        return carry

    leaving = []
    for i in range(GROUPS):
        lax.fori_loop(i * group, (i + 1) * group, one_peer, 0, unroll=2)
        at = pl.ds(i * group * cap, group * cap)
        copy = pltpu.make_async_copy(out_ref.at[at, :], out_hbm.at[at, :], out_sems.at[i])
        copy.start()
        leaving.append(copy)
    for copy in leaving:
        copy.wait()


def pick_donors(snapshots, send_list):
    peers, cap = send_list.shape
    snaps = snapshots.shape[1]
    hbm = pl.BlockSpec(memory_space=pltpu.HBM)
    dma = pltpu.SemaphoreType.DMA
    return pl.pallas_call(
        pick_kernel,
        out_shape=jax.ShapeDtypeStruct((peers * cap, snaps), F32),
        in_specs=[hbm, hbm],
        out_specs=hbm,
        scratch_shapes=[
            pltpu.VMEM(snapshots.shape, F32),
            pltpu.VMEM((peers * cap, snaps), F32),
            pltpu.SMEM(send_list.shape, jnp.int32),
            dma((PIECES,)),
            dma((GROUPS,)),
            dma(()),
        ],
        compiler_params=pltpu.CompilerParams(vmem_limit_bytes=MOST_VMEM),
        name="pick_donors",
    )(send_list, snapshots)


def weave_kernel(runs, run_rows, cap, peers, me_ref, sten_ref, wt_ref, mat_ref, slot_ref):
    step = pl.program_id(0)
    iota = lax.broadcasted_iota(jnp.int32, (cap, run_rows), 0)
    for sub in range(runs):
        run = step * runs + sub
        peer = lax.rem(me_ref[0] + run, peers)
        cols = slice(sub * run_rows, (sub + 1) * run_rows)
        dense = jnp.zeros((cap, run_rows), F32)
        for s in range(sten_ref.shape[0]):
            place = jnp.broadcast_to(sten_ref[s : s + 1, cols] - peer * cap, (cap, run_rows))
            value = jnp.broadcast_to(wt_ref[s : s + 1, cols], (cap, run_rows))
            dense = dense + jnp.where(iota == place, value, 0.0)
        high = dense.astype(BF16)
        high_f = high.astype(F32)
        low_f = (dense - high_f).astype(BF16).astype(F32)
        pair = jnp.concatenate([high_f, low_f], axis=0)
        mat = pair.T.astype(BF16)
        mat_ref[cols, :] = mat
        gram = jnp.dot(pair.astype(BF16), mat, preferred_element_type=F32)
        half = gram[:cap] + gram[cap:]
        slot_ref[sub * cap : (sub + 1) * cap, :] = half[:, :cap] + half[:, cap:]


def weave(me, stencil, weights, peers, cap):
    rows = stencil.shape[0]
    run_rows = rows // peers
    runs = max(1, 2048 // run_rows)
    block = runs * run_rows
    grid_spec = pltpu.PrefetchScalarGridSpec(
        num_scalar_prefetch=1,
        grid=(peers // runs,),
        in_specs=[
            pl.BlockSpec((stencil.shape[1], block), lambda i, m: (0, i)),
            pl.BlockSpec((stencil.shape[1], block), lambda i, m: (0, i)),
        ],
        out_specs=[
            pl.BlockSpec((block, 2 * cap), lambda i, m: (i, 0)),
            pl.BlockSpec((runs * cap, cap), lambda i, m: (i, 0)),
        ],
    )
    return pl.pallas_call(
        functools.partial(weave_kernel, runs, run_rows, cap, peers),
        out_shape=[jax.ShapeDtypeStruct((rows, 2 * cap), BF16), jax.ShapeDtypeStruct((peers * cap, cap), F32)],
        grid_spec=grid_spec,
        compiler_params=pltpu.CompilerParams(vmem_limit_bytes=16 * 1024 * 1024),
        cost_estimate=pl.CostEstimate(flops=8 * 10**9, bytes_accessed=40 * 10**6, transcendentals=0),
        name="weave",
    )(me, stencil.T, weights.T)


def two_sum(a, b):
    s = a + b
    t = s - a
    return s, (a - (s - t)) + (b - t)


def merge(a, b):
    s, e = two_sum(a[0], b[0])
    low = (a[1] + b[1]) + e
    high = s + low
    return high, low - (high - s)


def pack(full):
    size = full.shape[0]
    half, low = size // 2, 3 * size // 4
    lane = lax.broadcasted_iota(jnp.int32, (size // 4, size), 1)
    fold = jnp.where(lane < half, pltpu.roll(full[low:], half, 1), full[half:low])
    return jnp.concatenate([full[:half], fold], axis=0)


def unpack(packed):
    size = packed.shape[1]
    half = size // 2
    top, fold = packed[:half], packed[half:]
    lane = lax.broadcasted_iota(jnp.int32, (half, size), 1)
    corner = jnp.concatenate([fold, pltpu.roll(fold, half, 1)], axis=0)
    mirror = jnp.concatenate([top, top], axis=0).T[half:]
    return jnp.concatenate([top, jnp.where(lane < half, mirror, corner)], axis=0)


def gram_kernel(peers, cap, me_ref, x_ref, slot_ref, keep_ref, give_ref, z_ref):
    snaps = x_ref.shape[1]

    def one_run(run, carry):
        peer = lax.rem(me_ref[0] + run, peers)
        at = pl.ds(pl.multiple_of(peer * cap, cap), cap)
        frm = pl.ds(pl.multiple_of(run * cap, cap), cap)
        z_ref[at, :] = exact(slot_ref[frm, :], x_ref[at, :])
        return carry

    lax.fori_loop(0, peers, one_run, 0, unroll=16)
    chunk = 256

    def one_chunk(i, carry):
        at = pl.ds(pl.multiple_of(i * chunk, chunk), chunk)
        part = exact(x_ref[at, :], z_ref[at, :], ((0,), (0,)))
        s, e = two_sum(carry[0], part)
        return s, carry[1] + e

    zero = jnp.zeros((snaps, snaps), F32)
    high, low = lax.fori_loop(0, peers * cap // chunk, one_chunk, (zero, zero), unroll=8)
    core = lax.rem(me_ref[0], 2)
    half = keep_ref.shape[1]
    for i, part in enumerate((pack(high), pack(low))):
        keep_ref[i] = jnp.where(core == 0, part[:half], part[half:])
        give_ref[i] = jnp.where(core == 0, part[half:], part[:half])


def local_gram(me, x, slots, peers, cap):
    snaps = x.shape[1]
    shape = jax.ShapeDtypeStruct((2, 3 * snaps // 8, snaps), F32)
    vmem = pl.BlockSpec(memory_space=pltpu.VMEM)
    return pl.pallas_call(
        functools.partial(gram_kernel, peers, cap),
        out_shape=[shape, shape],
        in_specs=[pl.BlockSpec(memory_space=pltpu.SMEM), vmem, vmem],
        out_specs=[vmem, vmem],
        scratch_shapes=[pltpu.VMEM(x.shape, F32)],
        compiler_params=pltpu.CompilerParams(vmem_limit_bytes=limit((x.shape, F32), (x.shape, F32), (slots.shape, F32))),
        name="local_gram",
    )(me, x, slots)


def hop(value, mask, peers):
    return lax.ppermute(value, "rows", [(i, i ^ mask) for i in range(peers)])


def sum_pairs(keep, give, peers):
    other = hop(give, 1, peers)
    mine = merge((keep[0], keep[1]), (other[0], other[1]))
    bit = 2
    while bit < peers:
        now = jnp.stack(mine)
        if bit * 2 < peers:
            a = hop(now, bit, peers)
            b = hop(now, 2 * bit, peers)
            c = hop(now, 3 * bit, peers)
            mine = merge(merge(mine, (a[0], a[1])), merge((b[0], b[1]), (c[0], c[1])))
            bit *= 4
        else:
            a = hop(now, bit, peers)
            mine = merge(mine, (a[0], a[1]))
            bit *= 2
    now = jnp.stack(mine)
    return now, hop(now, 1, peers)


def power_scale(value):
    scale = jnp.ones_like(value)
    for k in (32, 16, 8, 4, 2, 1):
        small = value < 2.0 ** (2 - 2 * k)
        value = jnp.where(small, value * 2.0 ** (2 * k), value)
        scale = jnp.where(small, scale * 2.0**k, scale)
    for k in (32, 16, 8, 4, 2, 1):
        large = value >= 2.0 ** (2 * k)
        value = jnp.where(large, value * 2.0 ** (-2 * k), value)
        scale = jnp.where(large, scale * 2.0**-k, scale)
    return scale


def factor(gram):
    size = gram.shape[0]
    tile = (TILE, size)
    sub = lax.broadcasted_iota(jnp.int32, tile, 0)
    lane = lax.broadcasted_iota(jnp.int32, tile, 1)
    left = gram
    tops, inverses = [], []
    for j in range(size // TILE):
        rest = left.shape[0] - TILE
        many = rest // TILE
        columns = [left[:, j * TILE + k : j * TILE + k + 1] for k in range(TILE)]
        heads = [jnp.broadcast_to(column[:TILE], tile) for column in columns]
        tails = [jnp.broadcast_to(column[TILE:], (rest, size)) for column in columns] if rest else []
        block = [[jnp.broadcast_to(heads[k][i : i + 1, :], tile) for k in range(i + 1)] for i in range(TILE)]
        rows = [jnp.broadcast_to(left[k : k + 1, :], tile) for k in range(TILE)]
        irows = [jnp.where(lane < j * TILE, rows[k], (lane == j * TILE + k).astype(F32)) for k in range(TILE)]
        over, coef = [], {}
        if rest:
            ahead = [tail[:TILE] for tail in tails]
            kept = (lane < j * TILE) | (lane >= (j + 1) * TILE)
            near = jnp.where(kept, left[TILE : 2 * TILE], 0.0)
            solved = []
        for k in range(0, TILE, 2):
            n = k + 1
            first, cross = block[k][k], block[n][k]
            det = first * block[n][n] - cross * cross
            over_first, over_det = 1.0 / first, 1.0 / det
            over += [over_first, first * over_det]
            block[n][n] = det * over_first
            both = over_first * over_det
            coef[n, k] = cross * over_first
            moved = {i: block[i][n] * first - block[i][k] * cross for i in range(n + 1, TILE)}
            for i in range(n + 1, TILE):
                for c in range(n + 1, i + 1):
                    block[i][c] = (block[i][c] - (block[i][k] * block[c][k]) * over_first) - (moved[i] * moved[c]) * both
            for i in range(n + 1, TILE):
                coef[i, k] = block[i][k] * over_first
                coef[i, n] = moved[i] * over_det
            for many_rows in (rows, irows, ahead) if rest else (rows, irows):
                many_rows[n] = many_rows[n] - coef[n, k] * many_rows[k]
                for i in range(n + 1, TILE):
                    many_rows[i] = many_rows[i] - (coef[i, k] * many_rows[k] + coef[i, n] * many_rows[n])
            if rest:
                for c in (k, n):
                    solved.append(jnp.where(lane < (j + 1) * TILE, irows[c], rows[c]) * over[c])
                    near = near - ahead[c] * solved[c]
        top, inverse, pivots = rows[0], irows[0], block[0][0]
        for k in range(1, TILE):
            top = jnp.where(sub == k, rows[k], top)
            inverse = jnp.where(sub == k, irows[k], inverse)
            pivots = jnp.where(sub == k, block[k][k], pivots)
        root = lax.rsqrt(pivots)
        tops.append(jnp.where(lane >= sub + j * TILE, top * root, 0.0))
        inverses.append(inverse * root)
        if many == 1:
            left = near
        elif rest:
            for k in reversed(range(TILE)):
                for i in range(k):
                    solved[i] = solved[i] - coef[k, i] * solved[k]
            more = many - 1
            left = jnp.where(jnp.concatenate([kept] * more, axis=0), left[2 * TILE :], 0.0)
            for k in range(TILE):
                left = left - tails[k][TILE:] * jnp.concatenate([solved[k]] * more, axis=0)
            left = jnp.concatenate([near, left], axis=0)
    return jnp.concatenate(tops, axis=0), jnp.concatenate(inverses, axis=0)


def slices(value):
    out = []
    for bits in (6, 14, 22, 30):
        big = 1.5 * 2.0 ** (23 - bits)
        piece = (value + big) - big
        value = value - piece
        out.append(piece.astype(BF16))
    return out


def triangular(high, low):
    size = high.shape[0]
    rows = lax.broadcasted_iota(jnp.int32, (size, size), 0)
    cols = lax.broadcasted_iota(jnp.int32, (size, size), 1)
    diagonal = jnp.where(rows == cols, high, 0.0)
    across = power_scale(jnp.sum(diagonal, axis=0, keepdims=True))
    down = power_scale(jnp.sum(diagonal, axis=1, keepdims=True))
    high = high * across * down
    low = low * across * down
    upper, inv_t = factor(high)
    up = slices(upper)
    lo = slices(upper.T)
    first = jnp.dot(lo[0], jnp.concatenate(up, axis=1), preferred_element_type=F32)
    second = jnp.dot(lo[1], jnp.concatenate(up[:3], axis=1), preferred_element_type=F32)
    third = jnp.dot(lo[2], jnp.concatenate(up[:2], axis=1), preferred_element_type=F32)
    fourth = jnp.dot(lo[3], up[0], preferred_element_type=F32)
    rest = high - first[:, :size]
    rest = rest - (first[:, size : 2 * size] + second[:, :size])
    rest = rest - second[:, size : 2 * size]
    rest = rest - (first[:, 2 * size : 3 * size] + third[:, :size])
    rest = rest + low
    rest = rest - ((first[:, 3 * size :] + fourth) + (second[:, 2 * size :] + third[:, size:]))
    inv = inv_t.T
    slip = jnp.where(rows <= cols, exact(upper, inv) - (rows == cols).astype(F32), 0.0)
    weight = jnp.where(rows < cols, 1.0, jnp.where(rows == cols, 0.5, 0.0))
    error = exact(exact(inv_t, rest), inv) + rough(slip, slip, ((0,), (0,)))
    shift = error * weight + slip
    shift = (error - rough(shift, shift, ((0,), (0,)))) * weight + slip
    square = rough(shift, shift)
    shift = (error - rough(shift, shift, ((0,), (0,)))) * weight + slip
    minus = square - shift
    minus = minus + rough(square, minus)
    inv = inv + exact(inv, minus)
    upper = upper + exact(shift - slip - rough(shift, slip), upper)
    return upper * (1.0 / across), inv * down


def thirds(value):
    high = value.astype(BF16)
    rest = value - high.astype(F32)
    middle = rest.astype(BF16)
    return high, middle, (rest - middle.astype(F32)).astype(BF16)


CHUNKS = 8


def basis_kernel(
    cap, peers, scale, me_ref, mine_ref, other_ref, x_ref, mat_hbm, out_hbm, r_ref, y_ref, mat_ref, out_ref, sems, in_sem
):
    slots, snaps = x_ref.shape
    fetch = pltpu.make_async_copy(mat_hbm, mat_ref, in_sem)
    fetch.start()
    core = lax.rem(me_ref[0], 2)
    parts = []
    for i in range(2):
        mine, other = mine_ref[i], other_ref[i]
        top = jnp.where(core == 0, mine, other)
        low = jnp.where(core == 0, other, mine)
        parts.append(unpack(jnp.concatenate([top, low], axis=0)))
    upper, inv = triangular(parts[0], parts[1])
    r_ref[...] = upper * (1.0 / scale)
    high, middle, low = thirds(inv * scale)
    wide = jnp.concatenate([high, middle], axis=1)
    wide = jnp.concatenate([wide, wide], axis=0)
    tall = jnp.concatenate([low, high], axis=0)
    chunk = 512

    def one_chunk(i, carry):
        at = pl.ds(pl.multiple_of(i * chunk, chunk), chunk)
        high, middle, low = thirds(x_ref[at, :])
        first = jnp.dot(jnp.concatenate([high, middle], axis=1), wide, preferred_element_type=F32)
        second = jnp.dot(jnp.concatenate([high, low], axis=1), tall, preferred_element_type=F32)
        y = first[:, :snaps] + (first[:, snaps:] + second)
        y_high = y.astype(BF16)
        y_ref[at, :snaps] = y_high
        y_ref[at, snaps:] = (y - y_high.astype(F32)).astype(BF16)
        return carry

    lax.fori_loop(0, slots // chunk, one_chunk, 0)
    fetch.wait()
    rows = mat_ref.shape[0]
    block = rows // CHUNKS
    run_rows = rows // peers
    runs = block // run_rows

    def send(i):
        at = pl.ds(pl.multiple_of(i * block, block), block)
        return pltpu.make_async_copy(out_ref.at[at, :], out_hbm.at[at, :], sems.at[i])

    def one_block(i, carry):
        for sub in range(runs):
            run = i * runs + sub
            peer = lax.rem(me_ref[0] + run, peers)
            both = y_ref[pl.ds(pl.multiple_of(peer * cap, cap), cap), :]
            both = jnp.concatenate([both, both], axis=0)
            at = pl.ds(pl.multiple_of(run * run_rows, run_rows), run_rows)
            twice = jnp.dot(mat_ref[at, :], both, preferred_element_type=F32)
            out_ref[at, :] = twice[:, :snaps] + twice[:, snaps:]
        send(i).start()
        return carry

    lax.fori_loop(0, CHUNKS, one_block, 0, unroll=True)

    def one_wait(i, carry):
        send(i).wait()
        return carry

    lax.fori_loop(0, CHUNKS, one_wait, 0, unroll=True)


def make_basis(me, mine, other, x, mat, peers, cap, total_rows):
    rows = mat.shape[0]
    slots, snaps = x.shape
    vmem = pl.BlockSpec(memory_space=pltpu.VMEM)
    hbm = pl.BlockSpec(memory_space=pltpu.HBM)
    held = [((slots, 2 * snaps), BF16), (mat.shape, BF16), ((rows, snaps), F32)]
    return pl.pallas_call(
        functools.partial(basis_kernel, cap, peers, math.sqrt(total_rows)),
        out_shape=[jax.ShapeDtypeStruct((rows, snaps), F32), jax.ShapeDtypeStruct((snaps, snaps), F32)],
        in_specs=[pl.BlockSpec(memory_space=pltpu.SMEM), vmem, vmem, vmem, hbm],
        out_specs=[hbm, vmem],
        scratch_shapes=[pltpu.VMEM(*h) for h in held] + [pltpu.SemaphoreType.DMA((CHUNKS,)), pltpu.SemaphoreType.DMA(())],
        compiler_params=pltpu.CompilerParams(vmem_limit_bytes=BASIS_VMEM),
        name="make_basis",
    )(me, mine, other, x, mat)


def body(snapshots, send_list, stencil, weights):
    peers, cap = send_list.shape
    total_rows = stencil.shape[0] * peers
    me = lax.axis_index("rows").astype(jnp.int32).reshape(1)
    outgoing = pick_donors(snapshots, send_list)
    x = lax.all_to_all(outgoing, "rows", split_axis=0, concat_axis=0, tiled=True)
    mat, slots = weave(me, stencil, weights, peers, cap)
    keep, give = local_gram(me, x, slots, peers, cap)
    mine, other = sum_pairs(keep, give, peers)
    basis, r_factor = make_basis(me, mine, other, x, mat, peers, cap, total_rows)
    return (basis, r_factor)


def solution(mesh):
    return jax.shard_map(
        body,
        mesh=mesh,
        in_specs=(P("rows", None), P("rows", None), P("rows", None), P("rows", None)),
        out_specs=(P("rows", None), P()),
        check_vma=False,
    )
```

```python
import functools
import math

import jax
import jax.numpy as jnp
from jax import lax
from jax.experimental import pallas as pl
from jax.experimental.pallas import tpu as pltpu
from jax.sharding import PartitionSpec as P

F32 = jnp.float32
BF16 = jnp.bfloat16
TILE = 8


def exact(left, right, dims=((1,), (0,))):
    return lax.dot_general(left, right, (dims, ((), ())), precision=lax.Precision.HIGHEST, preferred_element_type=F32)


def rough(left, right, dims=((1,), (0,))):
    return lax.dot_general(left.astype(BF16), right.astype(BF16), (dims, ((), ())), preferred_element_type=F32)


PIECES = 8
GROUPS = 4
MOST_VMEM = 58 * 1024 * 1024
BASIS_VMEM = 50 * 1024 * 1024


def limit(*arrays):
    total = 0
    for shape, dtype in arrays:
        lanes = -(-shape[-1] // 128) * 128
        total += math.prod(shape[:-1]) * lanes * jnp.dtype(dtype).itemsize
    return total + 8 * 1024 * 1024


def pick_kernel(send_hbm, snap_hbm, out_hbm, held_ref, out_ref, send_ref, sems, out_sems, list_sem):
    peers, cap = send_hbm.shape
    part = snap_hbm.shape[0] // PIECES
    listed = pltpu.make_async_copy(send_hbm, send_ref, list_sem)
    listed.start()
    copies = []
    for i in range(PIECES):
        at = pl.ds(i * part, part)
        copy = pltpu.make_async_copy(snap_hbm.at[at, :], held_ref.at[at, :], sems.at[i])
        copy.start()
        copies.append(copy)
    listed.wait()
    for copy in copies:
        copy.wait()
    group = peers // GROUPS

    def one_peer(peer, carry):
        base = peer * cap
        for slot in range(cap):
            node = send_ref[peer, slot]
            out_ref[pl.ds(base + slot, 1), :] = held_ref[pl.ds(node, 1), :]
        return carry

    leaving = []
    for i in range(GROUPS):
        lax.fori_loop(i * group, (i + 1) * group, one_peer, 0, unroll=2)
        at = pl.ds(i * group * cap, group * cap)
        copy = pltpu.make_async_copy(out_ref.at[at, :], out_hbm.at[at, :], out_sems.at[i])
        copy.start()
        leaving.append(copy)
    for copy in leaving:
        copy.wait()


def pick_donors(snapshots, send_list):
    peers, cap = send_list.shape
    snaps = snapshots.shape[1]
    hbm = pl.BlockSpec(memory_space=pltpu.HBM)
    dma = pltpu.SemaphoreType.DMA
    return pl.pallas_call(
        pick_kernel,
        out_shape=jax.ShapeDtypeStruct((peers * cap, snaps), F32),
        in_specs=[hbm, hbm],
        out_specs=hbm,
        scratch_shapes=[
            pltpu.VMEM(snapshots.shape, F32),
            pltpu.VMEM((peers * cap, snaps), F32),
            pltpu.SMEM(send_list.shape, jnp.int32),
            dma((PIECES,)),
            dma((GROUPS,)),
            dma(()),
        ],
        compiler_params=pltpu.CompilerParams(vmem_limit_bytes=MOST_VMEM),
        name="pick_donors",
    )(send_list, snapshots)


def weave_kernel(runs, run_rows, cap, peers, me_ref, sten_ref, wt_ref, mat_ref, slot_ref):
    step = pl.program_id(0)
    iota = lax.broadcasted_iota(jnp.int32, (cap, run_rows), 0)
    for sub in range(runs):
        run = step * runs + sub
        peer = lax.rem(me_ref[0] + run, peers)
        cols = slice(sub * run_rows, (sub + 1) * run_rows)
        dense = jnp.zeros((cap, run_rows), F32)
        for s in range(sten_ref.shape[0]):
            place = jnp.broadcast_to(sten_ref[s : s + 1, cols] - peer * cap, (cap, run_rows))
            value = jnp.broadcast_to(wt_ref[s : s + 1, cols], (cap, run_rows))
            dense = dense + jnp.where(iota == place, value, 0.0)
        high = dense.astype(BF16)
        high_f = high.astype(F32)
        low_f = (dense - high_f).astype(BF16).astype(F32)
        pair = jnp.concatenate([high_f, low_f], axis=0)
        mat = pair.T.astype(BF16)
        mat_ref[cols, :] = mat
        gram = jnp.dot(pair.astype(BF16), mat, preferred_element_type=F32)
        half = gram[:cap] + gram[cap:]
        slot_ref[sub * cap : (sub + 1) * cap, :] = half[:, :cap] + half[:, cap:]


def weave(me, stencil, weights, peers, cap):
    rows = stencil.shape[0]
    run_rows = rows // peers
    runs = max(1, 2048 // run_rows)
    block = runs * run_rows
    grid_spec = pltpu.PrefetchScalarGridSpec(
        num_scalar_prefetch=1,
        grid=(peers // runs,),
        in_specs=[
            pl.BlockSpec((stencil.shape[1], block), lambda i, m: (0, i)),
            pl.BlockSpec((stencil.shape[1], block), lambda i, m: (0, i)),
        ],
        out_specs=[
            pl.BlockSpec((block, 2 * cap), lambda i, m: (i, 0)),
            pl.BlockSpec((runs * cap, cap), lambda i, m: (i, 0)),
        ],
    )
    return pl.pallas_call(
        functools.partial(weave_kernel, runs, run_rows, cap, peers),
        out_shape=[jax.ShapeDtypeStruct((rows, 2 * cap), BF16), jax.ShapeDtypeStruct((peers * cap, cap), F32)],
        grid_spec=grid_spec,
        compiler_params=pltpu.CompilerParams(vmem_limit_bytes=16 * 1024 * 1024),
        cost_estimate=pl.CostEstimate(flops=8 * 10**9, bytes_accessed=40 * 10**6, transcendentals=0),
        name="weave",
    )(me, stencil.T, weights.T)


def two_sum(a, b):
    s = a + b
    t = s - a
    return s, (a - (s - t)) + (b - t)


def merge(a, b):
    s, e = two_sum(a[0], b[0])
    low = (a[1] + b[1]) + e
    high = s + low
    return high, low - (high - s)


def pack(full):
    size = full.shape[0]
    half, low = size // 2, 3 * size // 4
    lane = lax.broadcasted_iota(jnp.int32, (size // 4, size), 1)
    fold = jnp.where(lane < half, pltpu.roll(full[low:], half, 1), full[half:low])
    return jnp.concatenate([full[:half], fold], axis=0)


def unpack(packed):
    size = packed.shape[1]
    half = size // 2
    top, fold = packed[:half], packed[half:]
    lane = lax.broadcasted_iota(jnp.int32, (half, size), 1)
    corner = jnp.concatenate([fold, pltpu.roll(fold, half, 1)], axis=0)
    mirror = jnp.concatenate([top, top], axis=0).T[half:]
    return jnp.concatenate([top, jnp.where(lane < half, mirror, corner)], axis=0)


def gram_kernel(peers, cap, me_ref, x_ref, slot_ref, keep_ref, give_ref, z_ref):
    snaps = x_ref.shape[1]

    def one_run(run, carry):
        peer = lax.rem(me_ref[0] + run, peers)
        at = pl.ds(pl.multiple_of(peer * cap, cap), cap)
        frm = pl.ds(pl.multiple_of(run * cap, cap), cap)
        z_ref[at, :] = exact(slot_ref[frm, :], x_ref[at, :])
        return carry

    lax.fori_loop(0, peers, one_run, 0, unroll=16)
    chunk = 256

    def one_chunk(i, carry):
        at = pl.ds(pl.multiple_of(i * chunk, chunk), chunk)
        part = exact(x_ref[at, :], z_ref[at, :], ((0,), (0,)))
        s, e = two_sum(carry[0], part)
        return s, carry[1] + e

    zero = jnp.zeros((snaps, snaps), F32)
    high, low = lax.fori_loop(0, peers * cap // chunk, one_chunk, (zero, zero), unroll=8)
    core = lax.rem(me_ref[0], 2)
    half = keep_ref.shape[1]
    for i, part in enumerate((pack(high), pack(low))):
        keep_ref[i] = jnp.where(core == 0, part[:half], part[half:])
        give_ref[i] = jnp.where(core == 0, part[half:], part[:half])


def local_gram(me, x, slots, peers, cap):
    snaps = x.shape[1]
    shape = jax.ShapeDtypeStruct((2, 3 * snaps // 8, snaps), F32)
    vmem = pl.BlockSpec(memory_space=pltpu.VMEM)
    return pl.pallas_call(
        functools.partial(gram_kernel, peers, cap),
        out_shape=[shape, shape],
        in_specs=[pl.BlockSpec(memory_space=pltpu.SMEM), vmem, vmem],
        out_specs=[vmem, vmem],
        scratch_shapes=[pltpu.VMEM(x.shape, F32)],
        compiler_params=pltpu.CompilerParams(vmem_limit_bytes=limit((x.shape, F32), (x.shape, F32), (slots.shape, F32))),
        name="local_gram",
    )(me, x, slots)


def hop(value, mask, peers):
    return lax.ppermute(value, "rows", [(i, i ^ mask) for i in range(peers)])


def sum_pairs(keep, give, peers):
    other = hop(give, 1, peers)
    mine = merge((keep[0], keep[1]), (other[0], other[1]))
    bit = 2
    while bit < peers:
        now = jnp.stack(mine)
        if bit * 2 < peers:
            a = hop(now, bit, peers)
            b = hop(now, 2 * bit, peers)
            c = hop(now, 3 * bit, peers)
            mine = merge(merge(mine, (a[0], a[1])), merge((b[0], b[1]), (c[0], c[1])))
            bit *= 4
        else:
            a = hop(now, bit, peers)
            mine = merge(mine, (a[0], a[1]))
            bit *= 2
    now = jnp.stack(mine)
    return now, hop(now, 1, peers)


def power_scale(value):
    scale = jnp.ones_like(value)
    for k in (32, 16, 8, 4, 2, 1):
        small = value < 2.0 ** (2 - 2 * k)
        value = jnp.where(small, value * 2.0 ** (2 * k), value)
        scale = jnp.where(small, scale * 2.0**k, scale)
    for k in (32, 16, 8, 4, 2, 1):
        large = value >= 2.0 ** (2 * k)
        value = jnp.where(large, value * 2.0 ** (-2 * k), value)
        scale = jnp.where(large, scale * 2.0**-k, scale)
    return scale


def factor(gram):
    size = gram.shape[0]
    tile = (TILE, size)
    sub = lax.broadcasted_iota(jnp.int32, tile, 0)
    lane = lax.broadcasted_iota(jnp.int32, tile, 1)
    panels = size // TILE
    left = [gram[i * TILE : (i + 1) * TILE] for i in range(panels)]

    def across(value, col):
        return jnp.broadcast_to(value[:, col : col + 1], tile)

    def down(value, row):
        return jnp.broadcast_to(value[row : row + 1, :], tile)

    tops, inverses = [], []
    heads = [across(left[0], k) for k in range(TILE)]
    ahead = [across(left[1], k) for k in range(TILE)]
    for j in range(panels):
        start, stop = j * TILE, (j + 1) * TILE
        later = range(j + 1, panels)
        tails = {i: [across(left[i], start + k) for k in range(TILE)] for i in later if i > j + 1}
        near_heads = [across(left[j + 1], stop + c) for c in range(TILE)] if j + 1 < panels else []
        near_ahead = [across(left[j + 2], stop + c) for c in range(TILE)] if j + 2 < panels else []
        second = list(tails[j + 2]) if j + 2 < panels else []
        block = [[down(heads[k], i) for k in range(i + 1)] for i in range(TILE)]
        rows = [down(left[j], k) for k in range(TILE)]
        irows = [jnp.where(lane < start, rows[k], (lane == start + k).astype(F32)) for k in range(TILE)]
        kept = (lane < start) | (lane >= stop)
        groups = [g for g in (ahead, second, rows, irows) if g]
        over, coef, solved = [], {}, []
        for k in range(0, TILE, 2):
            n = k + 1
            first, cross = block[k][k], block[n][k]
            det = first * block[n][n] - cross * cross
            over_first, over_det = 1.0 / first, 1.0 / det
            over += [over_first, first * over_det]
            block[n][n] = det * over_first
            both = over_first * over_det
            coef[n, k] = cross * over_first
            moved = {i: block[i][n] * first - block[i][k] * cross for i in range(n + 1, TILE)}
            for i in range(n + 1, TILE):
                for c in range(n + 1, i + 1):
                    block[i][c] = (block[i][c] - (block[i][k] * block[c][k]) * over_first) - (moved[i] * moved[c]) * both
            for i in range(n + 1, TILE):
                coef[i, k] = block[i][k] * over_first
                coef[i, n] = moved[i] * over_det
            for group in groups:
                group[n] = group[n] - coef[n, k] * group[k]
                for i in range(n + 1, TILE):
                    group[i] = group[i] - (coef[i, k] * group[k] + coef[i, n] * group[n])
            shrunk = {p: ahead[p] * over[p] for p in (k, n)} if near_heads else {}
            for c in range(TILE):
                for p in (k, n):
                    if near_heads:
                        scaled = down(shrunk[p], c)
                        near_heads[c] = near_heads[c] - ahead[p] * scaled
                    if near_ahead:
                        near_ahead[c] = near_ahead[c] - second[p] * scaled
            for p in (k, n):
                solved.append(jnp.where(lane < stop, irows[p], rows[p]) * over[p])
        top, inverse, pivots = rows[0], irows[0], block[0][0]
        for k in range(1, TILE):
            top = jnp.where(sub == k, rows[k], top)
            inverse = jnp.where(sub == k, irows[k], inverse)
            pivots = jnp.where(sub == k, block[k][k], pivots)
        root = lax.rsqrt(pivots)
        tops.append(jnp.where(lane >= sub + start, top * root, 0.0))
        inverses.append(inverse * root)
        for i, columns in ((j + 1, ahead), (j + 2, second)):
            if columns:
                value = jnp.where(kept, left[i], 0.0)
                for k in range(TILE):
                    value = value - columns[k] * solved[k]
                left[i] = value
        if j + 3 < panels:
            for k in reversed(range(TILE)):
                for i in range(k):
                    solved[i] = solved[i] - coef[k, i] * solved[k]
            for i in range(j + 3, panels):
                value = jnp.where(kept, left[i], 0.0)
                for k in range(TILE):
                    value = value - tails[i][k] * solved[k]
                left[i] = value
        heads, ahead = near_heads, near_ahead
    return jnp.concatenate(tops, axis=0), jnp.concatenate(inverses, axis=0)


def slices(value):
    out = []
    for bits in (6, 14, 22, 30):
        big = 1.5 * 2.0 ** (23 - bits)
        piece = (value + big) - big
        value = value - piece
        out.append(piece.astype(BF16))
    return out


def triangular(high, low):
    size = high.shape[0]
    rows = lax.broadcasted_iota(jnp.int32, (size, size), 0)
    cols = lax.broadcasted_iota(jnp.int32, (size, size), 1)
    diagonal = jnp.where(rows == cols, high, 0.0)
    across = power_scale(jnp.sum(diagonal, axis=0, keepdims=True))
    down = power_scale(jnp.sum(diagonal, axis=1, keepdims=True))
    high = high * across * down
    low = low * across * down
    upper, inv_t = factor(high)
    up = slices(upper)
    lo = slices(upper.T)
    first = jnp.dot(lo[0], jnp.concatenate(up, axis=1), preferred_element_type=F32)
    second = jnp.dot(lo[1], jnp.concatenate(up, axis=1), preferred_element_type=F32)
    third = jnp.dot(lo[2], jnp.concatenate(up[:3], axis=1), preferred_element_type=F32)
    fourth = jnp.dot(lo[3], jnp.concatenate(up[:2], axis=1), preferred_element_type=F32)
    part = lambda value, i: value[:, i * size : (i + 1) * size]
    rest = high - part(first, 0)
    rest = rest - (part(first, 1) + part(second, 0))
    rest = rest - part(second, 1)
    rest = rest - (part(first, 2) + part(third, 0))
    rest = rest + low
    rest = rest - ((part(first, 3) + part(fourth, 0)) + (part(second, 2) + part(third, 1)))
    rest = rest - ((part(second, 3) + part(fourth, 1)) + part(third, 2))
    inv = inv_t.T
    slip = jnp.where(rows <= cols, exact(upper, inv) - (rows == cols).astype(F32), 0.0)
    weight = jnp.where(rows < cols, 1.0, jnp.where(rows == cols, 0.5, 0.0))
    error = exact(exact(inv_t, rest), inv) + rough(slip, slip, ((0,), (0,)))
    shift = error * weight + slip
    shift = (error - rough(shift, shift, ((0,), (0,)))) * weight + slip
    square = rough(shift, shift)
    shift = (error - rough(shift, shift, ((0,), (0,)))) * weight + slip
    minus = square - shift
    minus = minus + rough(square, minus)
    inv = inv + exact(inv, minus)
    upper = upper + exact(shift - slip - rough(shift, slip), upper)
    return upper * (1.0 / across), inv * down


def thirds(value):
    high = value.astype(BF16)
    rest = value - high.astype(F32)
    middle = rest.astype(BF16)
    return high, middle, (rest - middle.astype(F32)).astype(BF16)


CHUNKS = 8


def basis_kernel(
    cap, peers, scale, me_ref, mine_ref, other_ref, x_ref, mat_hbm, out_hbm, r_ref, y_ref, mat_ref, out_ref, sems, in_sem
):
    slots, snaps = x_ref.shape
    fetch = pltpu.make_async_copy(mat_hbm, mat_ref, in_sem)
    fetch.start()
    core = lax.rem(me_ref[0], 2)
    parts = []
    for i in range(2):
        mine, other = mine_ref[i], other_ref[i]
        top = jnp.where(core == 0, mine, other)
        low = jnp.where(core == 0, other, mine)
        parts.append(unpack(jnp.concatenate([top, low], axis=0)))
    upper, inv = triangular(parts[0], parts[1])
    r_ref[...] = upper * (1.0 / scale)
    high, middle, low = thirds(inv * scale)
    wide = jnp.concatenate([high, middle], axis=1)
    wide = jnp.concatenate([wide, wide], axis=0)
    tall = jnp.concatenate([low, high], axis=0)
    chunk = 512

    def one_chunk(i, carry):
        at = pl.ds(pl.multiple_of(i * chunk, chunk), chunk)
        high, middle, low = thirds(x_ref[at, :])
        first = jnp.dot(jnp.concatenate([high, middle], axis=1), wide, preferred_element_type=F32)
        second = jnp.dot(jnp.concatenate([high, low], axis=1), tall, preferred_element_type=F32)
        y = first[:, :snaps] + (first[:, snaps:] + second)
        y_high = y.astype(BF16)
        y_ref[at, :snaps] = y_high
        y_ref[at, snaps:] = (y - y_high.astype(F32)).astype(BF16)
        return carry

    lax.fori_loop(0, slots // chunk, one_chunk, 0)
    fetch.wait()
    rows = mat_ref.shape[0]
    block = rows // CHUNKS
    run_rows = rows // peers
    runs = block // run_rows

    def send(i):
        at = pl.ds(pl.multiple_of(i * block, block), block)
        return pltpu.make_async_copy(out_ref.at[at, :], out_hbm.at[at, :], sems.at[i])

    def one_block(i, carry):
        for sub in range(runs):
            run = i * runs + sub
            peer = lax.rem(me_ref[0] + run, peers)
            both = y_ref[pl.ds(pl.multiple_of(peer * cap, cap), cap), :]
            both = jnp.concatenate([both, both], axis=0)
            at = pl.ds(pl.multiple_of(run * run_rows, run_rows), run_rows)
            twice = jnp.dot(mat_ref[at, :], both, preferred_element_type=F32)
            out_ref[at, :] = twice[:, :snaps] + twice[:, snaps:]
        send(i).start()
        return carry

    lax.fori_loop(0, CHUNKS, one_block, 0, unroll=True)

    def one_wait(i, carry):
        send(i).wait()
        return carry

    lax.fori_loop(0, CHUNKS, one_wait, 0, unroll=True)


def make_basis(me, mine, other, x, mat, peers, cap, total_rows):
    rows = mat.shape[0]
    slots, snaps = x.shape
    vmem = pl.BlockSpec(memory_space=pltpu.VMEM)
    hbm = pl.BlockSpec(memory_space=pltpu.HBM)
    held = [((slots, 2 * snaps), BF16), (mat.shape, BF16), ((rows, snaps), F32)]
    return pl.pallas_call(
        functools.partial(basis_kernel, cap, peers, math.sqrt(total_rows)),
        out_shape=[jax.ShapeDtypeStruct((rows, snaps), F32), jax.ShapeDtypeStruct((snaps, snaps), F32)],
        in_specs=[pl.BlockSpec(memory_space=pltpu.SMEM), vmem, vmem, vmem, hbm],
        out_specs=[hbm, vmem],
        scratch_shapes=[pltpu.VMEM(*h) for h in held] + [pltpu.SemaphoreType.DMA((CHUNKS,)), pltpu.SemaphoreType.DMA(())],
        compiler_params=pltpu.CompilerParams(vmem_limit_bytes=BASIS_VMEM),
        name="make_basis",
    )(me, mine, other, x, mat)


def body(snapshots, send_list, stencil, weights):
    peers, cap = send_list.shape
    total_rows = stencil.shape[0] * peers
    me = lax.axis_index("rows").astype(jnp.int32).reshape(1)
    outgoing = pick_donors(snapshots, send_list)
    x = lax.all_to_all(outgoing, "rows", split_axis=0, concat_axis=0, tiled=True)
    mat, slots = weave(me, stencil, weights, peers, cap)
    keep, give = local_gram(me, x, slots, peers, cap)
    mine, other = sum_pairs(keep, give, peers)
    basis, r_factor = make_basis(me, mine, other, x, mat, peers, cap, total_rows)
    return (basis, r_factor)


def solution(mesh):
    return jax.shard_map(
        body,
        mesh=mesh,
        in_specs=(P("rows", None), P("rows", None), P("rows", None), P("rows", None)),
        out_specs=(P("rows", None), P()),
        check_vma=False,
    )
```

```python
import functools
import math

import jax
import jax.numpy as jnp
from jax import lax
from jax.experimental import pallas as pl
from jax.experimental.pallas import tpu as pltpu
from jax.sharding import PartitionSpec as P

F32 = jnp.float32
BF16 = jnp.bfloat16
TILE = 8


def exact(left, right, dims=((1,), (0,))):
    return lax.dot_general(left, right, (dims, ((), ())), precision=lax.Precision.HIGHEST, preferred_element_type=F32)


def rough(left, right, dims=((1,), (0,))):
    return lax.dot_general(left.astype(BF16), right.astype(BF16), (dims, ((), ())), preferred_element_type=F32)


def thirds(value):
    high = value.astype(BF16)
    rest = value - high.astype(F32)
    middle = rest.astype(BF16)
    return high, middle, (rest - middle.astype(F32)).astype(BF16)


CHUNKS = 8


PIECES = 8
GROUPS = 4
MOST_VMEM = 58 * 1024 * 1024
BASIS_VMEM = 50 * 1024 * 1024


def limit(*arrays):
    total = 0
    for shape, dtype in arrays:
        lanes = -(-shape[-1] // 128) * 128
        total += math.prod(shape[:-1]) * lanes * jnp.dtype(dtype).itemsize
    return total + 8 * 1024 * 1024


def pick_kernel(send_hbm, snap_hbm, out_hbm, held_ref, out_ref, send_ref, sems, out_sems, list_sem):
    peers, cap = send_hbm.shape
    part = snap_hbm.shape[0] // PIECES
    listed = pltpu.make_async_copy(send_hbm, send_ref, list_sem)
    listed.start()
    copies = []
    for i in range(PIECES):
        at = pl.ds(i * part, part)
        copy = pltpu.make_async_copy(snap_hbm.at[at, :], held_ref.at[at, :], sems.at[i])
        copy.start()
        copies.append(copy)
    listed.wait()
    for copy in copies:
        copy.wait()
    group = peers // GROUPS

    def one_peer(peer, carry):
        base = peer * cap
        for slot in range(cap):
            node = send_ref[peer, slot]
            out_ref[pl.ds(base + slot, 1), :] = held_ref[pl.ds(node, 1), :]
        return carry

    leaving = []
    for i in range(GROUPS):
        lax.fori_loop(i * group, (i + 1) * group, one_peer, 0, unroll=2)
        at = pl.ds(i * group * cap, group * cap)
        copy = pltpu.make_async_copy(out_ref.at[at, :], out_hbm.at[at, :], out_sems.at[i])
        copy.start()
        leaving.append(copy)
    for copy in leaving:
        copy.wait()


def pick_donors(snapshots, send_list):
    peers, cap = send_list.shape
    snaps = snapshots.shape[1]
    hbm = pl.BlockSpec(memory_space=pltpu.HBM)
    dma = pltpu.SemaphoreType.DMA
    return pl.pallas_call(
        pick_kernel,
        out_shape=jax.ShapeDtypeStruct((peers * cap, snaps), F32),
        in_specs=[hbm, hbm],
        out_specs=hbm,
        scratch_shapes=[
            pltpu.VMEM(snapshots.shape, F32),
            pltpu.VMEM((peers * cap, snaps), F32),
            pltpu.SMEM(send_list.shape, jnp.int32),
            dma((PIECES,)),
            dma((GROUPS,)),
            dma(()),
        ],
        compiler_params=pltpu.CompilerParams(vmem_limit_bytes=MOST_VMEM),
        name="pick_donors",
    )(send_list, snapshots)


def weave_kernel(runs, run_rows, cap, peers, me_ref, sten_ref, wt_ref, mat_ref, slot_ref):
    step = pl.program_id(0)
    iota = lax.broadcasted_iota(jnp.int32, (cap, run_rows), 0)
    for sub in range(runs):
        run = step * runs + sub
        peer = lax.rem(me_ref[0] + run, peers)
        cols = slice(sub * run_rows, (sub + 1) * run_rows)
        dense = jnp.zeros((cap, run_rows), F32)
        for s in range(sten_ref.shape[0]):
            place = jnp.broadcast_to(sten_ref[s : s + 1, cols] - peer * cap, (cap, run_rows))
            value = jnp.broadcast_to(wt_ref[s : s + 1, cols], (cap, run_rows))
            dense = dense + jnp.where(iota == place, value, 0.0)
        high = dense.astype(BF16)
        high_f = high.astype(F32)
        low_f = (dense - high_f).astype(BF16).astype(F32)
        pair = jnp.concatenate([high_f, low_f], axis=0)
        mat = pair.T.astype(BF16)
        mat_ref[cols, :] = mat
        gram = jnp.dot(pair.astype(BF16), mat, preferred_element_type=F32)
        half = gram[:cap] + gram[cap:]
        s_high, s_middle, s_low = thirds(half[:, :cap] + half[:, cap:])
        slot_ref[sub * cap : (sub + 1) * cap, :] = jnp.concatenate([s_high, s_middle, s_low, s_high], axis=1)


def weave(me, stencil, weights, peers, cap):
    rows = stencil.shape[0]
    run_rows = rows // peers
    runs = max(1, 2048 // run_rows)
    block = runs * run_rows
    grid_spec = pltpu.PrefetchScalarGridSpec(
        num_scalar_prefetch=1,
        grid=(peers // runs,),
        in_specs=[
            pl.BlockSpec((stencil.shape[1], block), lambda i, m: (0, i)),
            pl.BlockSpec((stencil.shape[1], block), lambda i, m: (0, i)),
        ],
        out_specs=[
            pl.BlockSpec((block, 2 * cap), lambda i, m: (i, 0)),
            pl.BlockSpec((runs * cap, 4 * cap), lambda i, m: (i, 0)),
        ],
    )
    return pl.pallas_call(
        functools.partial(weave_kernel, runs, run_rows, cap, peers),
        out_shape=[jax.ShapeDtypeStruct((rows, 2 * cap), BF16), jax.ShapeDtypeStruct((peers * cap, 4 * cap), BF16)],
        grid_spec=grid_spec,
        compiler_params=pltpu.CompilerParams(vmem_limit_bytes=16 * 1024 * 1024),
        cost_estimate=pl.CostEstimate(flops=8 * 10**9, bytes_accessed=40 * 10**6, transcendentals=0),
        name="weave",
    )(me, stencil.T, weights.T)


def two_sum(a, b):
    s = a + b
    t = s - a
    return s, (a - (s - t)) + (b - t)


def merge(a, b):
    s, e = two_sum(a[0], b[0])
    low = (a[1] + b[1]) + e
    high = s + low
    return high, low - (high - s)


def pack(full):
    size = full.shape[0]
    half, low = size // 2, 3 * size // 4
    lane = lax.broadcasted_iota(jnp.int32, (size // 4, size), 1)
    fold = jnp.where(lane < half, pltpu.roll(full[low:], half, 1), full[half:low])
    return jnp.concatenate([full[:half], fold], axis=0)


def unpack(packed):
    size = packed.shape[1]
    half = size // 2
    top, fold = packed[:half], packed[half:]
    lane = lax.broadcasted_iota(jnp.int32, (half, size), 1)
    corner = jnp.concatenate([fold, pltpu.roll(fold, half, 1)], axis=0)
    mirror = jnp.concatenate([top, top], axis=0).T[half:]
    return jnp.concatenate([top, jnp.where(lane < half, mirror, corner)], axis=0)


def gram_kernel(peers, cap, me_ref, x_ref, slot_ref, keep_ref, give_ref, z_ref):
    snaps = x_ref.shape[1]

    def one_run(run, carry):
        peer = lax.rem(me_ref[0] + run, peers)
        at = pl.ds(pl.multiple_of(peer * cap, cap), cap)
        frm = pl.ds(pl.multiple_of(run * cap, cap), cap)
        high, middle, low = thirds(x_ref[at, :])
        wide = jnp.concatenate([high, middle], axis=1)
        last = jnp.concatenate([low, jnp.zeros_like(low)], axis=1)
        many = jnp.dot(
            slot_ref[frm, :],
            jnp.concatenate([wide, wide, wide, last], axis=0),
            preferred_element_type=F32,
        )
        z_ref[at, :] = many[:, :snaps] + many[:, snaps:]
        return carry

    lax.fori_loop(0, peers, one_run, 0, unroll=16)
    chunk = 256

    def one_chunk(i, carry):
        at = pl.ds(pl.multiple_of(i * chunk, chunk), chunk)
        part = exact(x_ref[at, :], z_ref[at, :], ((0,), (0,)))
        s, e = two_sum(carry[0], part)
        return s, carry[1] + e

    zero = jnp.zeros((snaps, snaps), F32)
    high, low = lax.fori_loop(0, peers * cap // chunk, one_chunk, (zero, zero), unroll=8)
    core = lax.rem(me_ref[0], 2)
    half = keep_ref.shape[1]
    for i, part in enumerate((pack(high), pack(low))):
        keep_ref[i] = jnp.where(core == 0, part[:half], part[half:])
        give_ref[i] = jnp.where(core == 0, part[half:], part[:half])


def local_gram(me, x, slots, peers, cap):
    snaps = x.shape[1]
    shape = jax.ShapeDtypeStruct((2, 3 * snaps // 8, snaps), F32)
    vmem = pl.BlockSpec(memory_space=pltpu.VMEM)
    return pl.pallas_call(
        functools.partial(gram_kernel, peers, cap),
        out_shape=[shape, shape],
        in_specs=[pl.BlockSpec(memory_space=pltpu.SMEM), vmem, vmem],
        out_specs=[vmem, vmem],
        scratch_shapes=[pltpu.VMEM(x.shape, F32)],
        compiler_params=pltpu.CompilerParams(vmem_limit_bytes=limit((x.shape, F32), (x.shape, F32), (slots.shape, BF16))),
        name="local_gram",
    )(me, x, slots)


def hop(value, mask, peers):
    return lax.ppermute(value, "rows", [(i, i ^ mask) for i in range(peers)])


def sum_pairs(keep, give, peers):
    other = hop(give, 1, peers)
    mine = merge((keep[0], keep[1]), (other[0], other[1]))
    bit = 2
    while bit < peers:
        now = jnp.stack(mine)
        if bit * 2 < peers:
            a = hop(now, bit, peers)
            b = hop(now, 2 * bit, peers)
            c = hop(now, 3 * bit, peers)
            mine = merge(merge(mine, (a[0], a[1])), merge((b[0], b[1]), (c[0], c[1])))
            bit *= 4
        else:
            a = hop(now, bit, peers)
            mine = merge(mine, (a[0], a[1]))
            bit *= 2
    now = jnp.stack(mine)
    return now, hop(now, 1, peers)


def power_scale(value):
    scale = jnp.ones_like(value)
    for k in (32, 16, 8, 4, 2, 1):
        small = value < 2.0 ** (2 - 2 * k)
        value = jnp.where(small, value * 2.0 ** (2 * k), value)
        scale = jnp.where(small, scale * 2.0**k, scale)
    for k in (32, 16, 8, 4, 2, 1):
        large = value >= 2.0 ** (2 * k)
        value = jnp.where(large, value * 2.0 ** (-2 * k), value)
        scale = jnp.where(large, scale * 2.0**-k, scale)
    return scale


def factor(gram):
    size = gram.shape[0]
    tile = (TILE, size)
    sub = lax.broadcasted_iota(jnp.int32, tile, 0)
    lane = lax.broadcasted_iota(jnp.int32, tile, 1)
    panels = size // TILE
    left = [gram[i * TILE : (i + 1) * TILE] for i in range(panels)]

    def across(value, col):
        return jnp.broadcast_to(value[:, col : col + 1], tile)

    def down(value, row):
        return jnp.broadcast_to(value[row : row + 1, :], tile)

    tops, inverses = [], []
    heads = [across(left[0], k) for k in range(TILE)]
    for j in range(panels):
        start, stop = j * TILE, (j + 1) * TILE
        later = range(j + 1, panels)
        tails = {i: [across(left[i], start + k) for k in range(TILE)] for i in later if i > j + 1}
        near_heads = [across(left[j + 1], stop + c) for c in range(TILE)] if j + 1 < panels else []
        ahead = [across(left[j + 1], start + k) for k in range(TILE)] if j + 1 < panels else []
        block = [[down(heads[k], i) for k in range(i + 1)] for i in range(TILE)]
        rows = [down(left[j], k) for k in range(TILE)]
        irows = [jnp.where(lane < start, rows[k], (lane == start + k).astype(F32)) for k in range(TILE)]
        kept = (lane < start) | (lane >= stop)
        groups = [g for g in (ahead, rows, irows) if g]
        over, coef, solved = [], {}, []
        for k in range(0, TILE, 2):
            n = k + 1
            first, cross = block[k][k], block[n][k]
            det = first * block[n][n] - cross * cross
            over_first, over_det = 1.0 / first, 1.0 / det
            over += [over_first, first * over_det]
            block[n][n] = det * over_first
            both = over_first * over_det
            coef[n, k] = cross * over_first
            moved = {i: block[i][n] * first - block[i][k] * cross for i in range(n + 1, TILE)}
            for i in range(n + 1, TILE):
                for c in range(n + 1, i + 1):
                    block[i][c] = (block[i][c] - (block[i][k] * block[c][k]) * over_first) - (moved[i] * moved[c]) * both
            for i in range(n + 1, TILE):
                coef[i, k] = block[i][k] * over_first
                coef[i, n] = moved[i] * over_det
            for group in groups:
                group[n] = group[n] - coef[n, k] * group[k]
                for i in range(n + 1, TILE):
                    group[i] = group[i] - (coef[i, k] * group[k] + coef[i, n] * group[n])
            shrunk = {p: ahead[p] * over[p] for p in (k, n)} if near_heads else {}
            for c in range(TILE):
                for p in (k, n):
                    if near_heads:
                        scaled = down(shrunk[p], c)
                        near_heads[c] = near_heads[c] - ahead[p] * scaled
            for p in (k, n):
                solved.append(jnp.where(lane < stop, irows[p], rows[p]) * over[p])
        top, inverse, pivots = rows[0], irows[0], block[0][0]
        for k in range(1, TILE):
            top = jnp.where(sub == k, rows[k], top)
            inverse = jnp.where(sub == k, irows[k], inverse)
            pivots = jnp.where(sub == k, block[k][k], pivots)
        root = lax.rsqrt(pivots)
        tops.append(jnp.where(lane >= sub + start, top * root, 0.0))
        inverses.append(inverse * root)
        if ahead:
            value = jnp.where(kept, left[j + 1], 0.0)
            for k in range(TILE):
                value = value - ahead[k] * solved[k]
            left[j + 1] = value
        if j + 2 < panels:
            for k in reversed(range(TILE)):
                for i in range(k):
                    solved[i] = solved[i] - coef[k, i] * solved[k]
            for i in range(j + 2, panels):
                value = jnp.where(kept, left[i], 0.0)
                for k in range(TILE):
                    value = value - tails[i][k] * solved[k]
                left[i] = value
        heads = near_heads
    return jnp.concatenate(tops, axis=0), jnp.concatenate(inverses, axis=0)


def slices(value):
    out = []
    for bits in (6, 14, 22, 30):
        big = 1.5 * 2.0 ** (23 - bits)
        piece = (value + big) - big
        value = value - piece
        out.append(piece.astype(BF16))
    return out


def triangular(high, low):
    size = high.shape[0]
    rows = lax.broadcasted_iota(jnp.int32, (size, size), 0)
    cols = lax.broadcasted_iota(jnp.int32, (size, size), 1)
    diagonal = jnp.where(rows == cols, high, 0.0)
    across = power_scale(jnp.sum(diagonal, axis=0, keepdims=True))
    down = power_scale(jnp.sum(diagonal, axis=1, keepdims=True))
    high = high * across * down
    low = low * across * down
    upper, inv_t = factor(high)
    up = slices(upper)
    lo = slices(upper.T)
    first = jnp.dot(lo[0], jnp.concatenate(up, axis=1), preferred_element_type=F32)
    second = jnp.dot(lo[1], jnp.concatenate(up, axis=1), preferred_element_type=F32)
    third = jnp.dot(lo[2], jnp.concatenate(up[:3], axis=1), preferred_element_type=F32)
    fourth = jnp.dot(lo[3], jnp.concatenate(up[:2], axis=1), preferred_element_type=F32)
    part = lambda value, i: value[:, i * size : (i + 1) * size]
    rest = high - part(first, 0)
    rest = rest - (part(first, 1) + part(second, 0))
    rest = rest - part(second, 1)
    rest = rest - (part(first, 2) + part(third, 0))
    rest = rest + low
    rest = rest - ((part(first, 3) + part(fourth, 0)) + (part(second, 2) + part(third, 1)))
    rest = rest - ((part(second, 3) + part(fourth, 1)) + part(third, 2))
    inv = inv_t.T
    slip = jnp.where(rows <= cols, exact(upper, inv) - (rows == cols).astype(F32), 0.0)
    weight = jnp.where(rows < cols, 1.0, jnp.where(rows == cols, 0.5, 0.0))
    error = exact(exact(inv_t, rest), inv) + rough(slip, slip, ((0,), (0,)))
    shift = error * weight + slip
    shift = (error - rough(shift, shift, ((0,), (0,)))) * weight + slip
    square = rough(shift, shift)
    shift = (error - rough(shift, shift, ((0,), (0,)))) * weight + slip
    minus = square - shift
    minus = minus + rough(square, minus)
    inv = inv + exact(inv, minus)
    upper = upper + exact(shift - slip - rough(shift, slip), upper)
    return upper * (1.0 / across), inv * down


def basis_kernel(
    cap, peers, scale, me_ref, mine_ref, other_ref, x_ref, mat_hbm, out_hbm, r_ref, y_ref, mat_ref, out_ref, sems, in_sem
):
    slots, snaps = x_ref.shape
    fetch = pltpu.make_async_copy(mat_hbm, mat_ref, in_sem)
    fetch.start()
    core = lax.rem(me_ref[0], 2)
    parts = []
    for i in range(2):
        mine, other = mine_ref[i], other_ref[i]
        top = jnp.where(core == 0, mine, other)
        low = jnp.where(core == 0, other, mine)
        parts.append(unpack(jnp.concatenate([top, low], axis=0)))
    upper, inv = triangular(parts[0], parts[1])
    r_ref[...] = upper * (1.0 / scale)
    high, middle, low = thirds(inv * scale)
    wide = jnp.concatenate([high, middle], axis=1)
    wide = jnp.concatenate([wide, wide], axis=0)
    tall = jnp.concatenate([low, high], axis=0)
    chunk = 512

    def one_chunk(i, carry):
        at = pl.ds(pl.multiple_of(i * chunk, chunk), chunk)
        high, middle, low = thirds(x_ref[at, :])
        first = jnp.dot(jnp.concatenate([high, middle], axis=1), wide, preferred_element_type=F32)
        second = jnp.dot(jnp.concatenate([high, low], axis=1), tall, preferred_element_type=F32)
        y = first[:, :snaps] + (first[:, snaps:] + second)
        y_high = y.astype(BF16)
        y_ref[at, :snaps] = y_high
        y_ref[at, snaps:] = (y - y_high.astype(F32)).astype(BF16)
        return carry

    lax.fori_loop(0, slots // chunk, one_chunk, 0)
    fetch.wait()
    rows = mat_ref.shape[0]
    block = rows // CHUNKS
    run_rows = rows // peers
    runs = block // run_rows

    def send(i):
        at = pl.ds(pl.multiple_of(i * block, block), block)
        return pltpu.make_async_copy(out_ref.at[at, :], out_hbm.at[at, :], sems.at[i])

    def one_block(i, carry):
        for sub in range(runs):
            run = i * runs + sub
            peer = lax.rem(me_ref[0] + run, peers)
            both = y_ref[pl.ds(pl.multiple_of(peer * cap, cap), cap), :]
            both = jnp.concatenate([both, both], axis=0)
            at = pl.ds(pl.multiple_of(run * run_rows, run_rows), run_rows)
            twice = jnp.dot(mat_ref[at, :], both, preferred_element_type=F32)
            out_ref[at, :] = twice[:, :snaps] + twice[:, snaps:]
        send(i).start()
        return carry

    lax.fori_loop(0, CHUNKS, one_block, 0, unroll=True)

    def one_wait(i, carry):
        send(i).wait()
        return carry

    lax.fori_loop(0, CHUNKS, one_wait, 0, unroll=True)


def make_basis(me, mine, other, x, mat, peers, cap, total_rows):
    rows = mat.shape[0]
    slots, snaps = x.shape
    vmem = pl.BlockSpec(memory_space=pltpu.VMEM)
    hbm = pl.BlockSpec(memory_space=pltpu.HBM)
    held = [((slots, 2 * snaps), BF16), (mat.shape, BF16), ((rows, snaps), F32)]
    return pl.pallas_call(
        functools.partial(basis_kernel, cap, peers, math.sqrt(total_rows)),
        out_shape=[jax.ShapeDtypeStruct((rows, snaps), F32), jax.ShapeDtypeStruct((snaps, snaps), F32)],
        in_specs=[pl.BlockSpec(memory_space=pltpu.SMEM), vmem, vmem, vmem, hbm],
        out_specs=[hbm, vmem],
        scratch_shapes=[pltpu.VMEM(*h) for h in held] + [pltpu.SemaphoreType.DMA((CHUNKS,)), pltpu.SemaphoreType.DMA(())],
        compiler_params=pltpu.CompilerParams(vmem_limit_bytes=BASIS_VMEM),
        name="make_basis",
    )(me, mine, other, x, mat)


def body(snapshots, send_list, stencil, weights):
    peers, cap = send_list.shape
    total_rows = stencil.shape[0] * peers
    me = lax.axis_index("rows").astype(jnp.int32).reshape(1)
    outgoing = pick_donors(snapshots, send_list)
    x = lax.all_to_all(outgoing, "rows", split_axis=0, concat_axis=0, tiled=True)
    mat, slots = weave(me, stencil, weights, peers, cap)
    keep, give = local_gram(me, x, slots, peers, cap)
    mine, other = sum_pairs(keep, give, peers)
    basis, r_factor = make_basis(me, mine, other, x, mat, peers, cap, total_rows)
    return (basis, r_factor)


def solution(mesh):
    return jax.shard_map(
        body,
        mesh=mesh,
        in_specs=(P("rows", None), P("rows", None), P("rows", None), P("rows", None)),
        out_specs=(P("rows", None), P()),
        check_vma=False,
    )
```

```python
import functools
import math

import jax
import jax.numpy as jnp
from jax import lax
from jax.experimental import pallas as pl
from jax.experimental.pallas import tpu as pltpu
from jax.sharding import PartitionSpec as P

F32 = jnp.float32
BF16 = jnp.bfloat16
TILE = 8


def exact(left, right, dims=((1,), (0,))):
    return lax.dot_general(left, right, (dims, ((), ())), precision=lax.Precision.HIGHEST, preferred_element_type=F32)


def rough(left, right, dims=((1,), (0,))):
    return lax.dot_general(left.astype(BF16), right.astype(BF16), (dims, ((), ())), preferred_element_type=F32)


def thirds(value):
    high = value.astype(BF16)
    rest = value - high.astype(F32)
    middle = rest.astype(BF16)
    return high, middle, (rest - middle.astype(F32)).astype(BF16)


CHUNKS = 8


PIECES = 8
GROUPS = 4
MOST_VMEM = 58 * 1024 * 1024
BASIS_VMEM = 50 * 1024 * 1024


def limit(*arrays):
    total = 0
    for shape, dtype in arrays:
        lanes = -(-shape[-1] // 128) * 128
        total += math.prod(shape[:-1]) * lanes * jnp.dtype(dtype).itemsize
    return total + 8 * 1024 * 1024


def pick_kernel(send_hbm, snap_hbm, out_hbm, held_ref, out_ref, send_ref, sems, out_sems, list_sem):
    peers, cap = send_hbm.shape
    part = snap_hbm.shape[0] // PIECES
    listed = pltpu.make_async_copy(send_hbm, send_ref, list_sem)
    listed.start()
    copies = []
    for i in range(PIECES):
        at = pl.ds(i * part, part)
        copy = pltpu.make_async_copy(snap_hbm.at[at, :], held_ref.at[at, :], sems.at[i])
        copy.start()
        copies.append(copy)
    listed.wait()
    for copy in copies:
        copy.wait()
    group = peers // GROUPS

    def one_peer(peer, carry):
        base = peer * cap
        for slot in range(cap):
            node = send_ref[peer, slot]
            out_ref[pl.ds(base + slot, 1), :] = held_ref[pl.ds(node, 1), :]
        return carry

    leaving = []
    for i in range(GROUPS):
        lax.fori_loop(i * group, (i + 1) * group, one_peer, 0, unroll=8)
        at = pl.ds(i * group * cap, group * cap)
        copy = pltpu.make_async_copy(out_ref.at[at, :], out_hbm.at[at, :], out_sems.at[i])
        copy.start()
        leaving.append(copy)
    for copy in leaving:
        copy.wait()


def pick_donors(snapshots, send_list):
    peers, cap = send_list.shape
    snaps = snapshots.shape[1]
    hbm = pl.BlockSpec(memory_space=pltpu.HBM)
    dma = pltpu.SemaphoreType.DMA
    return pl.pallas_call(
        pick_kernel,
        out_shape=jax.ShapeDtypeStruct((peers * cap, snaps), F32),
        in_specs=[hbm, hbm],
        out_specs=hbm,
        scratch_shapes=[
            pltpu.VMEM(snapshots.shape, F32),
            pltpu.VMEM((peers * cap, snaps), F32),
            pltpu.SMEM(send_list.shape, jnp.int32),
            dma((PIECES,)),
            dma((GROUPS,)),
            dma(()),
        ],
        compiler_params=pltpu.CompilerParams(vmem_limit_bytes=MOST_VMEM),
        name="pick_donors",
    )(send_list, snapshots)


def weave_kernel(runs, run_rows, cap, peers, me_ref, sten_ref, wt_ref, mat_ref, slot_ref):
    step = pl.program_id(0)
    iota = lax.broadcasted_iota(jnp.int32, (cap, run_rows), 0)
    for sub in range(runs):
        run = step * runs + sub
        peer = lax.rem(me_ref[0] + run, peers)
        cols = slice(sub * run_rows, (sub + 1) * run_rows)
        dense = jnp.zeros((cap, run_rows), F32)
        for s in range(sten_ref.shape[0]):
            place = jnp.broadcast_to(sten_ref[s : s + 1, cols] - peer * cap, (cap, run_rows))
            value = jnp.broadcast_to(wt_ref[s : s + 1, cols], (cap, run_rows))
            dense = dense + jnp.where(iota == place, value, 0.0)
        high = dense.astype(BF16)
        high_f = high.astype(F32)
        low_f = (dense - high_f).astype(BF16).astype(F32)
        pair = jnp.concatenate([high_f, low_f], axis=0)
        mat = pair.T.astype(BF16)
        mat_ref[cols, :] = mat
        gram = jnp.dot(pair.astype(BF16), mat, preferred_element_type=F32)
        half = gram[:cap] + gram[cap:]
        s_high, s_middle, s_low = thirds(half[:, :cap] + half[:, cap:])
        slot_ref[sub * cap : (sub + 1) * cap, :] = jnp.concatenate([s_high, s_middle, s_low, s_high], axis=1)


def weave(me, stencil, weights, peers, cap):
    rows = stencil.shape[0]
    run_rows = rows // peers
    runs = max(1, 2048 // run_rows)
    block = runs * run_rows
    grid_spec = pltpu.PrefetchScalarGridSpec(
        num_scalar_prefetch=1,
        grid=(peers // runs,),
        in_specs=[
            pl.BlockSpec((stencil.shape[1], block), lambda i, m: (0, i)),
            pl.BlockSpec((stencil.shape[1], block), lambda i, m: (0, i)),
        ],
        out_specs=[
            pl.BlockSpec((block, 2 * cap), lambda i, m: (i, 0)),
            pl.BlockSpec((runs * cap, 4 * cap), lambda i, m: (i, 0)),
        ],
    )
    return pl.pallas_call(
        functools.partial(weave_kernel, runs, run_rows, cap, peers),
        out_shape=[jax.ShapeDtypeStruct((rows, 2 * cap), BF16), jax.ShapeDtypeStruct((peers * cap, 4 * cap), BF16)],
        grid_spec=grid_spec,
        compiler_params=pltpu.CompilerParams(vmem_limit_bytes=16 * 1024 * 1024),
        cost_estimate=pl.CostEstimate(flops=8 * 10**9, bytes_accessed=40 * 10**6, transcendentals=0),
        name="weave",
    )(me, stencil.T, weights.T)


def two_sum(a, b):
    s = a + b
    t = s - a
    return s, (a - (s - t)) + (b - t)


def merge(a, b):
    s, e = two_sum(a[0], b[0])
    low = (a[1] + b[1]) + e
    high = s + low
    return high, low - (high - s)


def pack(full):
    size = full.shape[0]
    half, low = size // 2, 3 * size // 4
    lane = lax.broadcasted_iota(jnp.int32, (size // 4, size), 1)
    fold = jnp.where(lane < half, pltpu.roll(full[low:], half, 1), full[half:low])
    return jnp.concatenate([full[:half], fold], axis=0)


def unpack(packed):
    size = packed.shape[1]
    half = size // 2
    top, fold = packed[:half], packed[half:]
    lane = lax.broadcasted_iota(jnp.int32, (half, size), 1)
    corner = jnp.concatenate([fold, pltpu.roll(fold, half, 1)], axis=0)
    mirror = jnp.concatenate([top, top], axis=0).T[half:]
    return jnp.concatenate([top, jnp.where(lane < half, mirror, corner)], axis=0)


def gram_kernel(peers, cap, me_ref, x_ref, slot_ref, keep_ref, give_ref, z_ref):
    snaps = x_ref.shape[1]

    def one_run(run, carry):
        peer = lax.rem(me_ref[0] + run, peers)
        at = pl.ds(pl.multiple_of(peer * cap, cap), cap)
        frm = pl.ds(pl.multiple_of(run * cap, cap), cap)
        high, middle, low = thirds(x_ref[at, :])
        wide = jnp.concatenate([high, middle], axis=1)
        last = jnp.concatenate([low, jnp.zeros_like(low)], axis=1)
        many = jnp.dot(
            slot_ref[frm, :],
            jnp.concatenate([wide, wide, wide, last], axis=0),
            preferred_element_type=F32,
        )
        z_ref[at, :] = many[:, :snaps] + many[:, snaps:]
        return carry

    lax.fori_loop(0, peers, one_run, 0, unroll=32)
    chunk = 256

    def one_chunk(i, carry):
        at = pl.ds(pl.multiple_of(i * chunk, chunk), chunk)
        part = exact(x_ref[at, :], z_ref[at, :], ((0,), (0,)))
        s, e = two_sum(carry[0], part)
        return s, carry[1] + e

    zero = jnp.zeros((snaps, snaps), F32)
    high, low = lax.fori_loop(0, peers * cap // chunk, one_chunk, (zero, zero), unroll=8)
    core = lax.rem(me_ref[0], 2)
    half = keep_ref.shape[1]
    for i, part in enumerate((pack(high), pack(low))):
        keep_ref[i] = jnp.where(core == 0, part[:half], part[half:])
        give_ref[i] = jnp.where(core == 0, part[half:], part[:half])


def local_gram(me, x, slots, peers, cap):
    snaps = x.shape[1]
    shape = jax.ShapeDtypeStruct((2, 3 * snaps // 8, snaps), F32)
    vmem = pl.BlockSpec(memory_space=pltpu.VMEM)
    return pl.pallas_call(
        functools.partial(gram_kernel, peers, cap),
        out_shape=[shape, shape],
        in_specs=[pl.BlockSpec(memory_space=pltpu.SMEM), vmem, vmem],
        out_specs=[vmem, vmem],
        scratch_shapes=[pltpu.VMEM(x.shape, F32)],
        compiler_params=pltpu.CompilerParams(vmem_limit_bytes=limit((x.shape, F32), (x.shape, F32), (slots.shape, BF16))),
        name="local_gram",
    )(me, x, slots)


def hop(value, mask, peers):
    return lax.ppermute(value, "rows", [(i, i ^ mask) for i in range(peers)])


def sum_pairs(keep, give, peers):
    other = hop(give, 1, peers)
    mine = merge((keep[0], keep[1]), (other[0], other[1]))
    bit = 2
    while bit < peers:
        now = jnp.stack(mine)
        if bit * 2 < peers:
            a = hop(now, bit, peers)
            b = hop(now, 2 * bit, peers)
            c = hop(now, 3 * bit, peers)
            mine = merge(merge(mine, (a[0], a[1])), merge((b[0], b[1]), (c[0], c[1])))
            bit *= 4
        else:
            a = hop(now, bit, peers)
            mine = merge(mine, (a[0], a[1]))
            bit *= 2
    now = jnp.stack(mine)
    return now, hop(now, 1, peers)


def power_scale(value):
    scale = jnp.ones_like(value)
    for k in (32, 16, 8, 4, 2, 1):
        small = value < 2.0 ** (2 - 2 * k)
        value = jnp.where(small, value * 2.0 ** (2 * k), value)
        scale = jnp.where(small, scale * 2.0**k, scale)
    for k in (32, 16, 8, 4, 2, 1):
        large = value >= 2.0 ** (2 * k)
        value = jnp.where(large, value * 2.0 ** (-2 * k), value)
        scale = jnp.where(large, scale * 2.0**-k, scale)
    return scale


def factor(gram):
    size = gram.shape[0]
    tile = (TILE, size)
    sub = lax.broadcasted_iota(jnp.int32, tile, 0)
    lane = lax.broadcasted_iota(jnp.int32, tile, 1)
    panels = size // TILE
    left = [gram[i * TILE : (i + 1) * TILE] for i in range(panels)]

    def across(value, col):
        return jnp.broadcast_to(value[:, col : col + 1], tile)

    def down(value, row):
        return jnp.broadcast_to(value[row : row + 1, :], tile)

    tops, inverses = [], []
    heads = [across(left[0], k) for k in range(TILE)]
    for j in range(panels):
        start, stop = j * TILE, (j + 1) * TILE
        later = range(j + 1, panels)
        tails = {i: [across(left[i], start + k) for k in range(TILE)] for i in later if i > j + 1}
        near_heads = [across(left[j + 1], stop + c) for c in range(TILE)] if j + 1 < panels else []
        ahead = [across(left[j + 1], start + k) for k in range(TILE)] if j + 1 < panels else []
        block = [[down(heads[k], i) for k in range(i + 1)] for i in range(TILE)]
        rows = [down(left[j], k) for k in range(TILE)]
        irows = [jnp.where(lane < start, rows[k], (lane == start + k).astype(F32)) for k in range(TILE)]
        kept = (lane < start) | (lane >= stop)
        groups = [g for g in (ahead, rows, irows) if g]
        over, coef, solved = [], {}, []
        for k in range(0, TILE, 2):
            n = k + 1
            first, cross = block[k][k], block[n][k]
            det = first * block[n][n] - cross * cross
            over_first, over_det = 1.0 / first, 1.0 / det
            over += [over_first, first * over_det]
            block[n][n] = det * over_first
            both = over_first * over_det
            coef[n, k] = cross * over_first
            moved = {i: block[i][n] * first - block[i][k] * cross for i in range(n + 1, TILE)}
            for i in range(n + 1, TILE):
                for c in range(n + 1, i + 1):
                    block[i][c] = (block[i][c] - (block[i][k] * block[c][k]) * over_first) - (moved[i] * moved[c]) * both
            for i in range(n + 1, TILE):
                coef[i, k] = block[i][k] * over_first
                coef[i, n] = moved[i] * over_det
            for group in groups:
                group[n] = group[n] - coef[n, k] * group[k]
                for i in range(n + 1, TILE):
                    group[i] = group[i] - (coef[i, k] * group[k] + coef[i, n] * group[n])
            shrunk = {p: ahead[p] * over[p] for p in (k, n)} if near_heads else {}
            for c in range(TILE):
                for p in (k, n):
                    if near_heads:
                        scaled = down(shrunk[p], c)
                        near_heads[c] = near_heads[c] - ahead[p] * scaled
            for p in (k, n):
                solved.append(jnp.where(lane < stop, irows[p], rows[p]) * over[p])
        top, inverse, pivots = rows[0], irows[0], block[0][0]
        for k in range(1, TILE):
            top = jnp.where(sub == k, rows[k], top)
            inverse = jnp.where(sub == k, irows[k], inverse)
            pivots = jnp.where(sub == k, block[k][k], pivots)
        root = lax.rsqrt(pivots)
        tops.append(jnp.where(lane >= sub + start, top * root, 0.0))
        inverses.append(inverse * root)
        if ahead:
            value = jnp.where(kept, left[j + 1], 0.0)
            for k in range(TILE):
                value = value - ahead[k] * solved[k]
            left[j + 1] = value
        if j + 2 < panels:
            for k in reversed(range(TILE)):
                for i in range(k):
                    solved[i] = solved[i] - coef[k, i] * solved[k]
            for i in range(j + 2, panels):
                value = jnp.where(kept, left[i], 0.0)
                for k in range(TILE):
                    value = value - tails[i][k] * solved[k]
                left[i] = value
        heads = near_heads
    return jnp.concatenate(tops, axis=0), jnp.concatenate(inverses, axis=0)


def slices(value):
    out = []
    for bits in (6, 14, 22, 30):
        big = 1.5 * 2.0 ** (23 - bits)
        piece = (value + big) - big
        value = value - piece
        out.append(piece.astype(BF16))
    return out


def triangular(high, low):
    size = high.shape[0]
    rows = lax.broadcasted_iota(jnp.int32, (size, size), 0)
    cols = lax.broadcasted_iota(jnp.int32, (size, size), 1)
    diagonal = jnp.where(rows == cols, high, 0.0)
    across = power_scale(jnp.sum(diagonal, axis=0, keepdims=True))
    down = power_scale(jnp.sum(diagonal, axis=1, keepdims=True))
    high = high * across * down
    low = low * across * down
    upper, inv_t = factor(high)
    up = slices(upper)
    lo = slices(upper.T)
    first = jnp.dot(lo[0], jnp.concatenate(up, axis=1), preferred_element_type=F32)
    second = jnp.dot(lo[1], jnp.concatenate(up, axis=1), preferred_element_type=F32)
    third = jnp.dot(lo[2], jnp.concatenate(up[:3], axis=1), preferred_element_type=F32)
    fourth = jnp.dot(lo[3], jnp.concatenate(up[:2], axis=1), preferred_element_type=F32)
    part = lambda value, i: value[:, i * size : (i + 1) * size]
    rest = high - part(first, 0)
    rest = rest - (part(first, 1) + part(second, 0))
    rest = rest - part(second, 1)
    rest = rest - (part(first, 2) + part(third, 0))
    rest = rest + low
    rest = rest - ((part(first, 3) + part(fourth, 0)) + (part(second, 2) + part(third, 1)))
    rest = rest - ((part(second, 3) + part(fourth, 1)) + part(third, 2))
    inv = inv_t.T
    slip = jnp.where(rows <= cols, exact(upper, inv) - (rows == cols).astype(F32), 0.0)
    weight = jnp.where(rows < cols, 1.0, jnp.where(rows == cols, 0.5, 0.0))
    error = exact(exact(inv_t, rest), inv) + rough(slip, slip, ((0,), (0,)))
    shift = error * weight + slip
    shift = (error - rough(shift, shift, ((0,), (0,)))) * weight + slip
    square = rough(shift, shift)
    shift = (error - rough(shift, shift, ((0,), (0,)))) * weight + slip
    minus = square - shift
    minus = minus + rough(square, minus)
    inv = inv + exact(inv, minus)
    upper = upper + exact(shift - slip - rough(shift, slip), upper)
    return upper * (1.0 / across), inv * down


def basis_kernel(
    cap, peers, scale, me_ref, mine_ref, other_ref, x_ref, mat_hbm, out_hbm, r_ref, y_ref, mat_ref, out_ref, sems, in_sem
):
    slots, snaps = x_ref.shape
    fetch = pltpu.make_async_copy(mat_hbm, mat_ref, in_sem)
    fetch.start()
    core = lax.rem(me_ref[0], 2)
    parts = []
    for i in range(2):
        mine, other = mine_ref[i], other_ref[i]
        top = jnp.where(core == 0, mine, other)
        low = jnp.where(core == 0, other, mine)
        parts.append(unpack(jnp.concatenate([top, low], axis=0)))
    upper, inv = triangular(parts[0], parts[1])
    r_ref[...] = upper * (1.0 / scale)
    high, middle, low = thirds(inv * scale)
    wide = jnp.concatenate([high, middle], axis=1)
    wide = jnp.concatenate([wide, wide], axis=0)
    tall = jnp.concatenate([low, high], axis=0)
    chunk = 512

    def one_chunk(i, carry):
        at = pl.ds(pl.multiple_of(i * chunk, chunk), chunk)
        high, middle, low = thirds(x_ref[at, :])
        first = jnp.dot(jnp.concatenate([high, middle], axis=1), wide, preferred_element_type=F32)
        second = jnp.dot(jnp.concatenate([high, low], axis=1), tall, preferred_element_type=F32)
        y = first[:, :snaps] + (first[:, snaps:] + second)
        y_high = y.astype(BF16)
        y_ref[at, :snaps] = y_high
        y_ref[at, snaps:] = (y - y_high.astype(F32)).astype(BF16)
        return carry

    lax.fori_loop(0, slots // chunk, one_chunk, 0)
    fetch.wait()
    rows = mat_ref.shape[0]
    block = rows // CHUNKS
    run_rows = rows // peers
    runs = block // run_rows

    def send(i):
        at = pl.ds(pl.multiple_of(i * block, block), block)
        return pltpu.make_async_copy(out_ref.at[at, :], out_hbm.at[at, :], sems.at[i])

    def one_block(i, carry):
        for sub in range(runs):
            run = i * runs + sub
            peer = lax.rem(me_ref[0] + run, peers)
            both = y_ref[pl.ds(pl.multiple_of(peer * cap, cap), cap), :]
            both = jnp.concatenate([both, both], axis=0)
            at = pl.ds(pl.multiple_of(run * run_rows, run_rows), run_rows)
            twice = jnp.dot(mat_ref[at, :], both, preferred_element_type=F32)
            out_ref[at, :] = twice[:, :snaps] + twice[:, snaps:]
        send(i).start()
        return carry

    lax.fori_loop(0, CHUNKS, one_block, 0, unroll=True)

    def one_wait(i, carry):
        send(i).wait()
        return carry

    lax.fori_loop(0, CHUNKS, one_wait, 0, unroll=True)


def make_basis(me, mine, other, x, mat, peers, cap, total_rows):
    rows = mat.shape[0]
    slots, snaps = x.shape
    vmem = pl.BlockSpec(memory_space=pltpu.VMEM)
    hbm = pl.BlockSpec(memory_space=pltpu.HBM)
    held = [((slots, 2 * snaps), BF16), (mat.shape, BF16), ((rows, snaps), F32)]
    return pl.pallas_call(
        functools.partial(basis_kernel, cap, peers, math.sqrt(total_rows)),
        out_shape=[jax.ShapeDtypeStruct((rows, snaps), F32), jax.ShapeDtypeStruct((snaps, snaps), F32)],
        in_specs=[pl.BlockSpec(memory_space=pltpu.SMEM), vmem, vmem, vmem, hbm],
        out_specs=[hbm, vmem],
        scratch_shapes=[pltpu.VMEM(*h) for h in held] + [pltpu.SemaphoreType.DMA((CHUNKS,)), pltpu.SemaphoreType.DMA(())],
        compiler_params=pltpu.CompilerParams(vmem_limit_bytes=BASIS_VMEM),
        name="make_basis",
    )(me, mine, other, x, mat)


def body(snapshots, send_list, stencil, weights):
    peers, cap = send_list.shape
    total_rows = stencil.shape[0] * peers
    me = lax.axis_index("rows").astype(jnp.int32).reshape(1)
    outgoing = pick_donors(snapshots, send_list)
    x = lax.all_to_all(outgoing, "rows", split_axis=0, concat_axis=0, tiled=True)
    mat, slots = weave(me, stencil, weights, peers, cap)
    keep, give = local_gram(me, x, slots, peers, cap)
    mine, other = sum_pairs(keep, give, peers)
    basis, r_factor = make_basis(me, mine, other, x, mat, peers, cap, total_rows)
    return (basis, r_factor)


def solution(mesh):
    return jax.shard_map(
        body,
        mesh=mesh,
        in_specs=(P("rows", None), P("rows", None), P("rows", None), P("rows", None)),
        out_specs=(P("rows", None), P()),
        check_vma=False,
    )
```

```python
import functools
import math

import jax
import jax.numpy as jnp
from jax import lax
from jax.experimental import pallas as pl
from jax.experimental.pallas import tpu as pltpu
from jax.sharding import PartitionSpec as P

F32 = jnp.float32
BF16 = jnp.bfloat16
TILE = 8


def exact(left, right, dims=((1,), (0,))):
    return lax.dot_general(left, right, (dims, ((), ())), precision=lax.Precision.HIGHEST, preferred_element_type=F32)


def rough(left, right, dims=((1,), (0,))):
    return lax.dot_general(left.astype(BF16), right.astype(BF16), (dims, ((), ())), preferred_element_type=F32)


def thirds(value):
    high = value.astype(BF16)
    rest = value - high.astype(F32)
    middle = rest.astype(BF16)
    return high, middle, (rest - middle.astype(F32)).astype(BF16)


CHUNKS = 8


PIECES = 8
GROUPS = 4
MOST_VMEM = 58 * 1024 * 1024
BASIS_VMEM = 50 * 1024 * 1024


def limit(*arrays):
    total = 0
    for shape, dtype in arrays:
        lanes = -(-shape[-1] // 128) * 128
        total += math.prod(shape[:-1]) * lanes * jnp.dtype(dtype).itemsize
    return total + 8 * 1024 * 1024


def pick_kernel(send_hbm, snap_hbm, out_hbm, held_ref, out_ref, send_ref, sems, out_sems, list_sem):
    peers, cap = send_hbm.shape
    part = snap_hbm.shape[0] // PIECES
    listed = pltpu.make_async_copy(send_hbm, send_ref, list_sem)
    listed.start()
    copies = []
    for i in range(PIECES):
        at = pl.ds(i * part, part)
        copy = pltpu.make_async_copy(snap_hbm.at[at, :], held_ref.at[at, :], sems.at[i])
        copy.start()
        copies.append(copy)
    listed.wait()
    for copy in copies:
        copy.wait()
    group = peers // GROUPS

    def one_peer(peer, carry):
        base = peer * cap
        for slot in range(cap):
            node = send_ref[peer, slot]
            out_ref[pl.ds(base + slot, 1), :] = held_ref[pl.ds(node, 1), :]
        return carry

    leaving = []
    for i in range(GROUPS):
        lax.fori_loop(i * group, (i + 1) * group, one_peer, 0, unroll=8)
        at = pl.ds(i * group * cap, group * cap)
        copy = pltpu.make_async_copy(out_ref.at[at, :], out_hbm.at[at, :], out_sems.at[i])
        copy.start()
        leaving.append(copy)
    for copy in leaving:
        copy.wait()


def pick_donors(snapshots, send_list):
    peers, cap = send_list.shape
    snaps = snapshots.shape[1]
    hbm = pl.BlockSpec(memory_space=pltpu.HBM)
    dma = pltpu.SemaphoreType.DMA
    return pl.pallas_call(
        pick_kernel,
        out_shape=jax.ShapeDtypeStruct((peers * cap, snaps), F32),
        in_specs=[hbm, hbm],
        out_specs=hbm,
        scratch_shapes=[
            pltpu.VMEM(snapshots.shape, F32),
            pltpu.VMEM((peers * cap, snaps), F32),
            pltpu.SMEM(send_list.shape, jnp.int32),
            dma((PIECES,)),
            dma((GROUPS,)),
            dma(()),
        ],
        compiler_params=pltpu.CompilerParams(vmem_limit_bytes=MOST_VMEM),
        name="pick_donors",
    )(send_list, snapshots)


def weave_kernel(runs, run_rows, cap, peers, me_ref, sten_ref, wt_ref, mat_ref, slot_ref):
    step = pl.program_id(0)
    iota = lax.broadcasted_iota(jnp.int32, (cap, run_rows), 0)
    for sub in range(runs):
        run = step * runs + sub
        peer = lax.rem(me_ref[0] + run, peers)
        cols = slice(sub * run_rows, (sub + 1) * run_rows)
        dense = jnp.zeros((cap, run_rows), F32)
        for s in range(sten_ref.shape[0]):
            place = jnp.broadcast_to(sten_ref[s : s + 1, cols] - peer * cap, (cap, run_rows))
            value = jnp.broadcast_to(wt_ref[s : s + 1, cols], (cap, run_rows))
            dense = dense + jnp.where(iota == place, value, 0.0)
        high = dense.astype(BF16)
        high_f = high.astype(F32)
        low_f = (dense - high_f).astype(BF16).astype(F32)
        pair = jnp.concatenate([high_f, low_f], axis=0)
        mat = pair.T.astype(BF16)
        mat_ref[cols, :] = mat
        gram = jnp.dot(pair.astype(BF16), mat, preferred_element_type=F32)
        half = gram[:cap] + gram[cap:]
        s_high, s_middle, s_low = thirds(half[:, :cap] + half[:, cap:])
        slot_ref[sub * cap : (sub + 1) * cap, :] = jnp.concatenate([s_high, s_middle, s_low, s_high], axis=1)


def weave(me, stencil, weights, peers, cap):
    rows = stencil.shape[0]
    run_rows = rows // peers
    runs = max(1, 2048 // run_rows)
    block = runs * run_rows
    grid_spec = pltpu.PrefetchScalarGridSpec(
        num_scalar_prefetch=1,
        grid=(peers // runs,),
        in_specs=[
            pl.BlockSpec((stencil.shape[1], block), lambda i, m: (0, i)),
            pl.BlockSpec((stencil.shape[1], block), lambda i, m: (0, i)),
        ],
        out_specs=[
            pl.BlockSpec((block, 2 * cap), lambda i, m: (i, 0)),
            pl.BlockSpec((runs * cap, 4 * cap), lambda i, m: (i, 0)),
        ],
    )
    return pl.pallas_call(
        functools.partial(weave_kernel, runs, run_rows, cap, peers),
        out_shape=[jax.ShapeDtypeStruct((rows, 2 * cap), BF16), jax.ShapeDtypeStruct((peers * cap, 4 * cap), BF16)],
        grid_spec=grid_spec,
        compiler_params=pltpu.CompilerParams(vmem_limit_bytes=MOST_VMEM),
        cost_estimate=pl.CostEstimate(flops=8 * 10**9, bytes_accessed=40 * 10**6, transcendentals=0),
        name="weave",
    )(me, stencil.T, weights.T)


def two_sum(a, b):
    s = a + b
    t = s - a
    return s, (a - (s - t)) + (b - t)


def merge(a, b):
    s, e = two_sum(a[0], b[0])
    low = (a[1] + b[1]) + e
    high = s + low
    return high, low - (high - s)


def pack(full):
    size = full.shape[0]
    half, low = size // 2, 3 * size // 4
    lane = lax.broadcasted_iota(jnp.int32, (size // 4, size), 1)
    fold = jnp.where(lane < half, pltpu.roll(full[low:], half, 1), full[half:low])
    return jnp.concatenate([full[:half], fold], axis=0)


def unpack(packed):
    size = packed.shape[1]
    half = size // 2
    top, fold = packed[:half], packed[half:]
    lane = lax.broadcasted_iota(jnp.int32, (half, size), 1)
    corner = jnp.concatenate([fold, pltpu.roll(fold, half, 1)], axis=0)
    mirror = jnp.concatenate([top, top], axis=0).T[half:]
    return jnp.concatenate([top, jnp.where(lane < half, mirror, corner)], axis=0)


def gram_kernel(peers, cap, me_ref, x_ref, slot_ref, keep_ref, give_ref, z_ref):
    snaps = x_ref.shape[1]

    def one_run(run, carry):
        peer = lax.rem(me_ref[0] + run, peers)
        at = pl.ds(pl.multiple_of(peer * cap, cap), cap)
        frm = pl.ds(pl.multiple_of(run * cap, cap), cap)
        high, middle, low = thirds(x_ref[at, :])
        wide = jnp.concatenate([high, middle], axis=1)
        last = jnp.concatenate([low, jnp.zeros_like(low)], axis=1)
        many = jnp.dot(
            slot_ref[frm, :],
            jnp.concatenate([wide, wide, wide, last], axis=0),
            preferred_element_type=F32,
        )
        z_ref[at, :] = many[:, :snaps] + many[:, snaps:]
        return carry

    lax.fori_loop(0, peers, one_run, 0, unroll=32)
    chunk = 256

    def one_chunk(i, carry):
        at = pl.ds(pl.multiple_of(i * chunk, chunk), chunk)
        part = exact(x_ref[at, :], z_ref[at, :], ((0,), (0,)))
        s, e = two_sum(carry[0], part)
        return s, carry[1] + e

    zero = jnp.zeros((snaps, snaps), F32)
    high, low = lax.fori_loop(0, peers * cap // chunk, one_chunk, (zero, zero), unroll=8)
    core = lax.rem(me_ref[0], 2)
    half = keep_ref.shape[1]
    for i, part in enumerate((pack(high), pack(low))):
        keep_ref[i] = jnp.where(core == 0, part[:half], part[half:])
        give_ref[i] = jnp.where(core == 0, part[half:], part[:half])


def local_gram(me, x, slots, peers, cap):
    snaps = x.shape[1]
    shape = jax.ShapeDtypeStruct((2, 3 * snaps // 8, snaps), F32)
    vmem = pl.BlockSpec(memory_space=pltpu.VMEM)
    return pl.pallas_call(
        functools.partial(gram_kernel, peers, cap),
        out_shape=[shape, shape],
        in_specs=[pl.BlockSpec(memory_space=pltpu.SMEM), vmem, vmem],
        out_specs=[vmem, vmem],
        scratch_shapes=[pltpu.VMEM(x.shape, F32)],
        compiler_params=pltpu.CompilerParams(vmem_limit_bytes=limit((x.shape, F32), (x.shape, F32), (slots.shape, BF16))),
        name="local_gram",
    )(me, x, slots)


def hop(value, mask, peers):
    return lax.ppermute(value, "rows", [(i, i ^ mask) for i in range(peers)])


def sum_pairs(keep, give, peers):
    other = hop(give, 1, peers)
    mine = merge((keep[0], keep[1]), (other[0], other[1]))
    bit = 2
    while bit < peers:
        now = jnp.stack(mine)
        if bit * 2 < peers:
            a = hop(now, bit, peers)
            b = hop(now, 2 * bit, peers)
            c = hop(now, 3 * bit, peers)
            mine = merge(merge(mine, (a[0], a[1])), merge((b[0], b[1]), (c[0], c[1])))
            bit *= 4
        else:
            a = hop(now, bit, peers)
            mine = merge(mine, (a[0], a[1]))
            bit *= 2
    now = jnp.stack(mine)
    return now, hop(now, 1, peers)


def power_scale(value):
    scale = jnp.ones_like(value)
    for k in (32, 16, 8, 4, 2, 1):
        small = value < 2.0 ** (2 - 2 * k)
        value = jnp.where(small, value * 2.0 ** (2 * k), value)
        scale = jnp.where(small, scale * 2.0**k, scale)
    for k in (32, 16, 8, 4, 2, 1):
        large = value >= 2.0 ** (2 * k)
        value = jnp.where(large, value * 2.0 ** (-2 * k), value)
        scale = jnp.where(large, scale * 2.0**-k, scale)
    return scale


def factor(gram):
    size = gram.shape[0]
    tile = (TILE, size)
    sub = lax.broadcasted_iota(jnp.int32, tile, 0)
    lane = lax.broadcasted_iota(jnp.int32, tile, 1)
    panels = size // TILE
    left = [gram[i * TILE : (i + 1) * TILE] for i in range(panels)]

    def across(value, col):
        return jnp.broadcast_to(value[:, col : col + 1], tile)

    def down(value, row):
        return jnp.broadcast_to(value[row : row + 1, :], tile)

    tops, inverses = [], []
    heads = [across(left[0], k) for k in range(TILE)]
    for j in range(panels):
        start, stop = j * TILE, (j + 1) * TILE
        later = range(j + 1, panels)
        tails = {i: [across(left[i], start + k) for k in range(TILE)] for i in later if i > j + 1}
        near_heads = [across(left[j + 1], stop + c) for c in range(TILE)] if j + 1 < panels else []
        ahead = [across(left[j + 1], start + k) for k in range(TILE)] if j + 1 < panels else []
        block = [[down(heads[k], i) for k in range(i + 1)] for i in range(TILE)]
        rows = [down(left[j], k) for k in range(TILE)]
        irows = [jnp.where(lane < start, rows[k], (lane == start + k).astype(F32)) for k in range(TILE)]
        kept = (lane < start) | (lane >= stop)
        groups = [g for g in (ahead, rows, irows) if g]
        over, coef, solved = [], {}, []
        for k in range(0, TILE, 2):
            n = k + 1
            first, cross = block[k][k], block[n][k]
            det = first * block[n][n] - cross * cross
            over_first, over_det = 1.0 / first, 1.0 / det
            over += [over_first, first * over_det]
            block[n][n] = det * over_first
            both = over_first * over_det
            coef[n, k] = cross * over_first
            moved = {i: block[i][n] * first - block[i][k] * cross for i in range(n + 1, TILE)}
            for i in range(n + 1, TILE):
                for c in range(n + 1, i + 1):
                    block[i][c] = (block[i][c] - (block[i][k] * block[c][k]) * over_first) - (moved[i] * moved[c]) * both
            for i in range(n + 1, TILE):
                coef[i, k] = block[i][k] * over_first
                coef[i, n] = moved[i] * over_det
            for group in groups:
                group[n] = group[n] - coef[n, k] * group[k]
                for i in range(n + 1, TILE):
                    group[i] = group[i] - (coef[i, k] * group[k] + coef[i, n] * group[n])
            shrunk = {p: ahead[p] * over[p] for p in (k, n)} if near_heads else {}
            for c in range(TILE):
                for p in (k, n):
                    if near_heads:
                        scaled = down(shrunk[p], c)
                        near_heads[c] = near_heads[c] - ahead[p] * scaled
            for p in (k, n):
                solved.append(jnp.where(lane < stop, irows[p], rows[p]) * over[p])
        top, inverse, pivots = rows[0], irows[0], block[0][0]
        for k in range(1, TILE):
            top = jnp.where(sub == k, rows[k], top)
            inverse = jnp.where(sub == k, irows[k], inverse)
            pivots = jnp.where(sub == k, block[k][k], pivots)
        root = lax.rsqrt(pivots)
        tops.append(jnp.where(lane >= sub + start, top * root, 0.0))
        inverses.append(inverse * root)
        if ahead:
            value = jnp.where(kept, left[j + 1], 0.0)
            for k in range(TILE):
                value = value - ahead[k] * solved[k]
            left[j + 1] = value
        if j + 2 < panels:
            for k in reversed(range(TILE)):
                for i in range(k):
                    solved[i] = solved[i] - coef[k, i] * solved[k]
            for i in range(j + 2, panels):
                value = jnp.where(kept, left[i], 0.0)
                for k in range(TILE):
                    value = value - tails[i][k] * solved[k]
                left[i] = value
        heads = near_heads
    return jnp.concatenate(tops, axis=0), jnp.concatenate(inverses, axis=0)


def slices(value):
    out = []
    for bits in (6, 14, 22, 30):
        big = 1.5 * 2.0 ** (23 - bits)
        piece = (value + big) - big
        value = value - piece
        out.append(piece.astype(BF16))
    return out


def triangular(high, low):
    size = high.shape[0]
    rows = lax.broadcasted_iota(jnp.int32, (size, size), 0)
    cols = lax.broadcasted_iota(jnp.int32, (size, size), 1)
    diagonal = jnp.where(rows == cols, high, 0.0)
    across = power_scale(jnp.sum(diagonal, axis=0, keepdims=True))
    down = power_scale(jnp.sum(diagonal, axis=1, keepdims=True))
    high = high * across * down
    low = low * across * down
    upper, inv_t = factor(high)
    up = slices(upper)
    lo = slices(upper.T)
    first = jnp.dot(lo[0], jnp.concatenate(up, axis=1), preferred_element_type=F32)
    second = jnp.dot(lo[1], jnp.concatenate(up, axis=1), preferred_element_type=F32)
    third = jnp.dot(lo[2], jnp.concatenate(up[:3], axis=1), preferred_element_type=F32)
    fourth = jnp.dot(lo[3], jnp.concatenate(up[:2], axis=1), preferred_element_type=F32)
    part = lambda value, i: value[:, i * size : (i + 1) * size]
    rest = high - part(first, 0)
    rest = rest - (part(first, 1) + part(second, 0))
    rest = rest - part(second, 1)
    rest = rest - (part(first, 2) + part(third, 0))
    rest = rest + low
    rest = rest - ((part(first, 3) + part(fourth, 0)) + (part(second, 2) + part(third, 1)))
    rest = rest - ((part(second, 3) + part(fourth, 1)) + part(third, 2))
    inv = inv_t.T
    slip = jnp.where(rows <= cols, exact(upper, inv) - (rows == cols).astype(F32), 0.0)
    weight = jnp.where(rows < cols, 1.0, jnp.where(rows == cols, 0.5, 0.0))
    error = exact(exact(inv_t, rest), inv) + rough(slip, slip, ((0,), (0,)))
    shift = error * weight + slip
    shift = (error - rough(shift, shift, ((0,), (0,)))) * weight + slip
    square = rough(shift, shift)
    shift = (error - rough(shift, shift, ((0,), (0,)))) * weight + slip
    minus = square - shift
    minus = minus + rough(square, minus)
    inv = inv + exact(inv, minus)
    upper = upper + exact(shift - slip - rough(shift, slip), upper)
    return upper * (1.0 / across), inv * down


def basis_kernel(
    cap, peers, scale, me_ref, mine_ref, other_ref, x_ref, mat_hbm, out_hbm, r_ref, y_ref, mat_ref, out_ref, sems, in_sem
):
    slots, snaps = x_ref.shape
    fetch = pltpu.make_async_copy(mat_hbm, mat_ref, in_sem)
    fetch.start()
    core = lax.rem(me_ref[0], 2)
    parts = []
    for i in range(2):
        mine, other = mine_ref[i], other_ref[i]
        top = jnp.where(core == 0, mine, other)
        low = jnp.where(core == 0, other, mine)
        parts.append(unpack(jnp.concatenate([top, low], axis=0)))
    upper, inv = triangular(parts[0], parts[1])
    r_ref[...] = upper * (1.0 / scale)
    high, middle, low = thirds(inv * scale)
    wide = jnp.concatenate([high, middle], axis=1)
    wide = jnp.concatenate([wide, wide], axis=0)
    tall = jnp.concatenate([low, high], axis=0)
    chunk = 512

    def one_chunk(i, carry):
        at = pl.ds(pl.multiple_of(i * chunk, chunk), chunk)
        high, middle, low = thirds(x_ref[at, :])
        first = jnp.dot(jnp.concatenate([high, middle], axis=1), wide, preferred_element_type=F32)
        second = jnp.dot(jnp.concatenate([high, low], axis=1), tall, preferred_element_type=F32)
        y = first[:, :snaps] + (first[:, snaps:] + second)
        y_high = y.astype(BF16)
        y_ref[at, :snaps] = y_high
        y_ref[at, snaps:] = (y - y_high.astype(F32)).astype(BF16)
        return carry

    lax.fori_loop(0, slots // chunk, one_chunk, 0)
    fetch.wait()
    rows = mat_ref.shape[0]
    block = rows // CHUNKS
    run_rows = rows // peers
    runs = block // run_rows

    def send(i):
        at = pl.ds(pl.multiple_of(i * block, block), block)
        return pltpu.make_async_copy(out_ref.at[at, :], out_hbm.at[at, :], sems.at[i])

    def one_block(i, carry):
        for sub in range(runs):
            run = i * runs + sub
            peer = lax.rem(me_ref[0] + run, peers)
            both = y_ref[pl.ds(pl.multiple_of(peer * cap, cap), cap), :]
            both = jnp.concatenate([both, both], axis=0)
            at = pl.ds(pl.multiple_of(run * run_rows, run_rows), run_rows)
            twice = jnp.dot(mat_ref[at, :], both, preferred_element_type=F32)
            out_ref[at, :] = twice[:, :snaps] + twice[:, snaps:]
        send(i).start()
        return carry

    lax.fori_loop(0, CHUNKS, one_block, 0, unroll=True)

    def one_wait(i, carry):
        send(i).wait()
        return carry

    lax.fori_loop(0, CHUNKS, one_wait, 0, unroll=True)


def make_basis(me, mine, other, x, mat, peers, cap, total_rows):
    rows = mat.shape[0]
    slots, snaps = x.shape
    vmem = pl.BlockSpec(memory_space=pltpu.VMEM)
    hbm = pl.BlockSpec(memory_space=pltpu.HBM)
    held = [((slots, 2 * snaps), BF16), (mat.shape, BF16), ((rows, snaps), F32)]
    return pl.pallas_call(
        functools.partial(basis_kernel, cap, peers, math.sqrt(total_rows)),
        out_shape=[jax.ShapeDtypeStruct((rows, snaps), F32), jax.ShapeDtypeStruct((snaps, snaps), F32)],
        in_specs=[pl.BlockSpec(memory_space=pltpu.SMEM), vmem, vmem, vmem, hbm],
        out_specs=[hbm, vmem],
        scratch_shapes=[pltpu.VMEM(*h) for h in held] + [pltpu.SemaphoreType.DMA((CHUNKS,)), pltpu.SemaphoreType.DMA(())],
        compiler_params=pltpu.CompilerParams(vmem_limit_bytes=BASIS_VMEM),
        name="make_basis",
    )(me, mine, other, x, mat)


def body(snapshots, send_list, stencil, weights):
    peers, cap = send_list.shape
    total_rows = stencil.shape[0] * peers
    me = lax.axis_index("rows").astype(jnp.int32).reshape(1)
    outgoing = pick_donors(snapshots, send_list)
    x = lax.all_to_all(outgoing, "rows", split_axis=0, concat_axis=0, tiled=True)
    mat, slots = weave(me, stencil, weights, peers, cap)
    keep, give = local_gram(me, x, slots, peers, cap)
    mine, other = sum_pairs(keep, give, peers)
    basis, r_factor = make_basis(me, mine, other, x, mat, peers, cap, total_rows)
    return (basis, r_factor)


def solution(mesh):
    return jax.shard_map(
        body,
        mesh=mesh,
        in_specs=(P("rows", None), P("rows", None), P("rows", None), P("rows", None)),
        out_specs=(P("rows", None), P()),
        check_vma=False,
    )
```
